256 devices in a mesh: section: 4 (over z_lo), rep: 8 (over y, core), tp: 8 (over z_hi, x).
Axes of the slice: x: 4, y: 4, z: 8 (z_hi: 2, z_lo: 4; z = z_hi * 4 + z_lo), core: 2. Of those that a mesh axis runs over, the one named last changes fastest.
Arguments:
- acts: bfloat16 [8, 256, 896], P('rep', None, 'tp'), may hold values from -6 to 6
- cotangent: bfloat16 [8, 256, 896], P('rep', None, 'tp'), may hold values from -8.5 to 8.5
- w_gate: bfloat16 [4, 8, 896, 4864], P('section', 'rep', None, 'tp'), may hold values from -3 to 3
- w_up: bfloat16 [4, 8, 896, 4864], P('section', 'rep', None, 'tp'), may hold values from -3 to 3
- w_down: bfloat16 [4, 8, 4864, 896], P('section', 'rep', 'tp'), may hold values from -4.2 to 4.2
- m_gate: bfloat16 [4, 8, 896, 4864], P('section', 'rep', None, 'tp'), may hold values from -0.099609375 to 0.099609375
- m_up: bfloat16 [4, 8, 896, 4864], P('section', 'rep', None, 'tp'), may hold values from -0.099609375 to 0.099609375
- m_down: bfloat16 [4, 8, 4864, 896], P('section', 'rep', 'tp'), may hold values from -0.099609375 to 0.099609375
- v_gate: bfloat16 [4, 8, 896, 4864], P('section', 'rep', None, 'tp'), may hold values from 0.0009994507 to 0.099609375
- v_up: bfloat16 [4, 8, 896, 4864], P('section', 'rep', None, 'tp'), may hold values from 0.0009994507 to 0.099609375
- v_down: bfloat16 [4, 8, 4864, 896], P('section', 'rep', 'tp'), may hold values from 0.0009994507 to 0.099609375
- steps: int32 [4], P('section'), may hold values from 0 to 999
Outputs:
- section_out: bfloat16 [4, 8, 256, 896], P('section', 'rep', None, 'tp')
- section_in_grad: bfloat16 [4, 8, 256, 896], P('section', 'rep', None, 'tp')
- new_gate: bfloat16 [4, 8, 896, 4864], P('section', 'rep', None, 'tp')
- new_up: bfloat16 [4, 8, 896, 4864], P('section', 'rep', None, 'tp')
- new_down: bfloat16 [4, 8, 4864, 896], P('section', 'rep', 'tp')
The draws below stay inside these ranges and needn't reach their ends.
All inputs are finite; a program needn't handle non-finite values.
Results may differ from the reference program's by a relative error of at most 0.023.
Values may be sent and summed in bfloat16 or wider, within the bound.
A program may use at most 128 MiB of HBM per device.

```python
import math
import jax
import jax.numpy as jnp
from jax import lax

D = 896
FF = 4864
ROWS = 256
SECTIONS = 4
REPLICAS = 8
N_SECTION = 4
N_REP = 8


def noise_field(key, shape, bound):
    return jax.random.truncated_normal(key, -bound, bound, shape, jnp.float32)


def shared_acts(key):
    base = jax.random.fold_in(key, 11)
    shape = (REPLICAS, ROWS, D)
    values = noise_field(base, shape, 6.0)
    return values


def shared_up(key):
    base = jax.random.fold_in(key, 21)
    return noise_field(base, (SECTIONS, REPLICAS, D, FF), 3.0)


def draw_acts(key, part):
    return shared_acts(key).astype(jnp.bfloat16)


def draw_cotangent(key, part):
    common = shared_acts(key)
    extra = noise_field(jax.random.fold_in(key, 12), (REPLICAS, ROWS, D), 6.0)
    return (0.7 * common + 0.7 * extra).astype(jnp.bfloat16)


def draw_w_up(key, part):
    return shared_up(key).astype(jnp.bfloat16)


def draw_w_down(key, part):
    upper = shared_up(key)
    extra = noise_field(jax.random.fold_in(key, 22), (SECTIONS, REPLICAS, FF, D), 3.0)
    return (0.6 * jnp.swapaxes(upper, 2, 3) + 0.8 * extra).astype(jnp.bfloat16)


def touch_ends(entries, own_key, smallest, largest):
    place = [jax.random.randint(jax.random.fold_in(own_key, axis), (), 0, length) for axis, length in enumerate(entries.shape)]
    longest = entries.shape.index(max(entries.shape))
    next_to = place[:longest] + [(place[longest] + 1) % entries.shape[longest]] + place[longest + 1:]
    return entries.at[tuple(place)].set(smallest).at[tuple(next_to)].set(largest)


def block_levels(rng, shape, split, smallest, high):
    level = 1.0
    for axis_at, blocks in split:
        heights = jax.random.uniform(jax.random.fold_in(jax.random.fold_in(rng, 6), axis_at), (blocks,), jnp.float32, smallest / len(split), high / len(split))
        level = level * jnp.repeat(jnp.exp(heights), shape[axis_at] // blocks).reshape((-1,) + (1,) * (len(shape) - 1 - axis_at))
    return level


def gaussian(key, shape, scale, reach, split=(), held_as=jnp.bfloat16):
    array = scale * jax.random.normal(key, shape, jnp.float32)
    if split:
        array = array * block_levels(key, shape, split, -0.22, 0.18)
    return jnp.clip(array, -reach, reach).astype(held_as)


def setup_inputs(seed: int = 0) -> dict:
    key_of = jax.random.split(jax.random.key(seed), 13)
    return {
        "acts": draw_acts(jax.random.fold_in(key_of[12], 71), 0),
        "cotangent": draw_cotangent(jax.random.fold_in(key_of[12], 71), 0),
        "w_gate": gaussian(key_of[2], (SECTIONS, REPLICAS, D, FF), 1.0, 3.0, ((0, 4), (1, 8), (3, 8))),
        "w_up": draw_w_up(jax.random.fold_in(key_of[12], 71), 0),
        "w_down": draw_w_down(jax.random.fold_in(key_of[12], 71), 0),
        "m_gate": gaussian(key_of[5], (SECTIONS, REPLICAS, D, FF), 0.03, 0.099609375, ((0, 4), (1, 8), (3, 8))),
        "m_up": gaussian(key_of[6], (SECTIONS, REPLICAS, D, FF), 0.03, 0.099609375, ((0, 4), (1, 8), (3, 8))),
        "m_down": gaussian(key_of[7], (SECTIONS, REPLICAS, FF, D), 0.03, 0.099609375, ((0, 4), (1, 8), (2, 8))),
        "v_gate": jnp.clip(jnp.exp(math.log(0.099609375) - 4.6018058 * jax.random.uniform(key_of[8], (SECTIONS, REPLICAS, D, FF), jnp.float32) ** block_levels(key_of[8], (SECTIONS, REPLICAS, D, FF), ((0, 4), (1, 8), (3, 8)), -0.2, 0.2)), 0.0009994507, 0.099609375).astype(jnp.bfloat16),
        "v_up": jnp.clip(jnp.exp(math.log(0.099609375) - 4.6018058 * jax.random.uniform(key_of[9], (SECTIONS, REPLICAS, D, FF), jnp.float32) ** block_levels(key_of[9], (SECTIONS, REPLICAS, D, FF), ((0, 4), (1, 8), (3, 8)), -0.2, 0.2)), 0.0009994507, 0.099609375).astype(jnp.bfloat16),
        "v_down": jnp.clip(jnp.exp(math.log(0.099609375) - 4.6018058 * jax.random.uniform(key_of[10], (SECTIONS, REPLICAS, FF, D), jnp.float32) ** block_levels(key_of[10], (SECTIONS, REPLICAS, FF, D), ((0, 4), (1, 8), (2, 8)), -0.2, 0.2)), 0.0009994507, 0.099609375).astype(jnp.bfloat16),
        "steps": touch_ends(jax.random.randint(key_of[11], (SECTIONS,), 0, 1000), jax.random.fold_in(key_of[11], 1), 0, 999).astype(jnp.int32),
    }


NORM_EPS = 1e-06
ADAM_EPS = 1e-08
LEARN = 0.3
BETA_ONE = 0.9
BETA_TWO = 0.95

def forward_parts(x, wg, wu):
    xf = x.astype(jnp.float32)
    rms = jnp.sqrt(lax.optimization_barrier(jnp.mean(xf * xf, axis=1, keepdims=True)) + NORM_EPS)
    normed = xf / rms
    normed_b = normed.astype(jnp.bfloat16)
    gate = jnp.dot(normed_b, wg, preferred_element_type=jnp.float32) * (1.0 / math.sqrt(D))
    upper = jnp.dot(normed_b, wu, preferred_element_type=jnp.float32) * (1.0 / math.sqrt(D))
    return (xf, rms, normed, normed_b, gate, upper)

def adam_step(w, m, v, g):
    m_new = BETA_ONE * m.astype(jnp.float32) + (1.0 - BETA_ONE) * g
    v_new = BETA_TWO * v.astype(jnp.float32) + (1.0 - BETA_TWO) * g * g
    return (w.astype(jnp.float32) - LEARN * m_new / (jnp.sqrt(v_new) + ADAM_EPS)).astype(jnp.bfloat16)

def reference(acts, cotangent, w_gate, w_up, w_down, m_gate, m_up, m_down, v_gate, v_up, v_down, steps):
    outs_all = []
    grads_all = []
    gates_all = []
    ups_all = []
    downs_all = []
    for rep_idx in range(N_REP):
        inputs = []
        outputs = []
        x = acts[rep_idx]
        for section_idx in range(N_SECTION):
            inputs.append(x)
            xf, rms, normed, normed_b, gate, upper = forward_parts(x, w_gate[section_idx, rep_idx], w_up[section_idx, rep_idx])
            hidden = (jax.nn.silu(gate) * upper).astype(jnp.bfloat16)
            down = jnp.dot(hidden, w_down[section_idx, rep_idx], preferred_element_type=jnp.float32) * (1.0 / math.sqrt(FF))
            x = (xf + down).astype(jnp.bfloat16)
            outputs.append(x)
        in_grads = [None] * N_SECTION
        new_g = [None] * N_SECTION
        new_u = [None] * N_SECTION
        new_d = [None] * N_SECTION
        dy = cotangent[rep_idx]
        for section_idx in range(N_SECTION - 1, -1, -1):
            wg = w_gate[section_idx, rep_idx]
            wu = w_up[section_idx, rep_idx]
            wd = w_down[section_idx, rep_idx]
            xf, rms, normed, normed_b, gate, upper = forward_parts(inputs[section_idx], wg, wu)
            sig = jax.nn.sigmoid(gate)
            active = gate * sig
            hidden = (active * upper).astype(jnp.bfloat16)
            dh = jnp.dot(dy, wd.T, preferred_element_type=jnp.float32) * (1.0 / math.sqrt(FF))
            dgate = (dh * upper * sig * (1.0 + gate * (1.0 - sig))).astype(jnp.bfloat16)
            dup = (dh * active).astype(jnp.bfloat16)
            g_down = jnp.dot(hidden.T, dy, preferred_element_type=jnp.float32) * (1.0 / math.sqrt(FF))
            g_gate = jnp.dot(normed_b.T, dgate, preferred_element_type=jnp.float32) * (1.0 / math.sqrt(D))
            g_up = jnp.dot(normed_b.T, dup, preferred_element_type=jnp.float32) * (1.0 / math.sqrt(D))
            dnorm = (jnp.dot(dgate, wg.T, preferred_element_type=jnp.float32) + jnp.dot(dup, wu.T, preferred_element_type=jnp.float32)) * (1.0 / math.sqrt(D))
            stat = lax.optimization_barrier(jnp.sum(dnorm * normed, axis=1, keepdims=True)) / D
            dx = (dy.astype(jnp.float32) + (dnorm - normed * stat) / rms).astype(jnp.bfloat16)
            in_grads[section_idx] = dx
            new_g[section_idx] = adam_step(wg, m_gate[section_idx, rep_idx], v_gate[section_idx, rep_idx], g_gate)
            new_u[section_idx] = adam_step(wu, m_up[section_idx, rep_idx], v_up[section_idx, rep_idx], g_up)
            new_d[section_idx] = adam_step(wd, m_down[section_idx, rep_idx], v_down[section_idx, rep_idx], g_down)
            dy = dx
        outs_all.append(jnp.stack(outputs))
        grads_all.append(jnp.stack(in_grads))
        gates_all.append(jnp.stack(new_g))
        ups_all.append(jnp.stack(new_u))
        downs_all.append(jnp.stack(new_d))
    section_out = jnp.stack(outs_all, axis=1)
    section_in_grad = jnp.stack(grads_all, axis=1)
    updated = [jnp.stack(gates_all, axis=1), jnp.stack(ups_all, axis=1), jnp.stack(downs_all, axis=1)]
    levels = N_REP.bit_length() - 1
    results = []
    for weights in updated:
        rows = []
        for section_idx in range(N_SECTION):
            distance = jnp.left_shift(jnp.int32(1), (steps[section_idx] % levels).astype(jnp.int32))
            source = ((jnp.arange(N_REP, dtype=jnp.int32) - distance) % N_REP).astype(jnp.int32)
            partner = jnp.take(weights[section_idx], source, axis=0)
            rows.append(((weights[section_idx].astype(jnp.float32) + partner.astype(jnp.float32)) * 0.5).astype(jnp.bfloat16))
        results.append(jnp.stack(rows))
    return (section_out, section_in_grad, results[0], results[1], results[2])
```

```python
import functools
import math

import jax
import jax.numpy as jnp
from jax import lax
from jax.experimental import pallas as pl
from jax.experimental.pallas import tpu as pltpu
from jax.sharding import PartitionSpec as P

D = 896
FF = 4864
ROWS = 256
SECTIONS = 4
TP = 8
NX = 4
BLOCK = D // TP
MB = 2
R = ROWS // MB
C = R // NX

NORM_EPS = 1e-06
ADAM_EPS = 1e-08
LEARN = 0.3
BETA_ONE = 0.9
BETA_TWO = 0.95
INV_D = 1.0 / math.sqrt(D)
INV_FF = 1.0 / math.sqrt(FF)
MESH = pl.DeviceIdType.MESH
BF16 = jnp.bfloat16
F32 = jnp.float32

CODES = {"I": 0, "H": 1, "M": 2, "T": 3, "h": 4, "m": 5, "t": 6, "O": 7, "o": 8, "E": 9}


def plan(text):
    return [(CODES[name], int(mb)) for name, mb in zip(text[::2], text[1::2])]


EARLY = plan("I0H0M0H1T0M1T1O0O1h0m0h1t0m1t1o0o1E0")
LAST = plan("I0H0M0m0H1M1t0m1t1T0T1O0O1o0o1E0E1E1")


def rms_parts(rows):
    xf = rows.astype(F32)
    rms = jnp.sqrt(jnp.mean(xf * xf, axis=1, keepdims=True) + NORM_EPS)
    return xf, rms


def dot_nn(left, right):
    return lax.dot_general(left, right, (((1,), (0,)), ((), ())), preferred_element_type=F32)


def dot_nt(left, right):
    return lax.dot_general(left, right, (((1,), (1,)), ((), ())), preferred_element_type=F32)


def chain_kernel(
    acts,
    cot,
    wg,
    wu,
    wd,
    out_y,
    out_dx,
    out_nb,
    out_hidden,
    out_dgate,
    out_dup,
    out_dy,
    xin,
    full,
    act_s,
    slope_s,
    spread,
    nb,
    dyb,
    xrow,
    dyrow,
    part_f,
    part_b,
    rs_f,
    rs_b,
    zsend_f,
    zsend_b,
    zrecv_f,
    zrecv_b,
    zown_f,
    zown_b,
    ost_f,
    ost_b,
    orecv_f,
    orecv_b,
    in_send,
    in_recv,
    ag_send,
    ag_recv,
    rs_send,
    rs_recv,
    z_send,
    z_recv,
    o_send,
    o_recv,
):
    s = lax.axis_index("section")
    t = lax.axis_index("tp")
    h = t // NX
    x = t % NX
    own = pl.ds(pl.multiple_of(x * C, C), C)

    def at_tp(where):
        return {"tp": where}

    def peer_x(k):
        return (x + k) % NX

    barrier = pltpu.get_barrier_semaphore()
    for k in range(1, TP):
        pl.semaphore_signal(barrier, inc=1, device_id={"tp": (t + k) % TP}, device_id_type=MESH)
    for step in (1, SECTIONS - 1):
        for hh in range(2):
            pl.semaphore_signal(
                barrier,
                inc=1,
                device_id={"section": (s + step) % SECTIONS, "tp": hh * NX + x},
                device_id_type=MESH,
            )
    pl.semaphore_wait(barrier, TP - 1 + 4)

    def in_copy(src, k):
        return pltpu.make_async_remote_copy(
            src_ref=src,
            dst_ref=xin.at[t],
            send_sem=in_send.at[k],
            recv_sem=in_recv.at[t],
            device_id={"tp": (t + k) % TP},
            device_id_type=MESH,
        )

    def in_wait(k):
        who = (t + k) % TP
        pltpu.make_async_remote_copy(
            src_ref=xin.at[who],
            dst_ref=xin.at[who],
            send_sem=in_send.at[0],
            recv_sem=in_recv.at[who],
            device_id={"tp": who},
            device_id_type=MESH,
        ).wait_recv()

    order = (4, 5, 3, 6, 2, 7, 1)

    @pl.when(s == 0)
    def _():
        for k in order:
            in_copy(acts, k).start()

    @pl.when(s == SECTIONS - 1)
    def _():
        for k in order:
            in_copy(cot, k).start()

    def gather_blocks():
        for k in range(1, TP):
            in_wait(k)
        full[...] = jnp.concatenate([xin[k] for k in range(TP)], axis=1)

    def ag_copy(buf, kind, mb, k):
        return pltpu.make_async_remote_copy(
            src_ref=buf.at[mb, own],
            dst_ref=buf.at[mb, own],
            send_sem=ag_send.at[kind, mb, k],
            recv_sem=ag_recv.at[kind, mb, NX - k],
            device_id={"tp": h * NX + peer_x(k)},
            device_id_type=MESH,
        )

    def ag_wait(buf, kind, mb, k):
        rows = pl.ds(pl.multiple_of(peer_x(k) * C, C), C)
        pltpu.make_async_remote_copy(
            src_ref=buf.at[mb, rows],
            dst_ref=buf.at[mb, rows],
            send_sem=ag_send.at[kind, mb, k],
            recv_sem=ag_recv.at[kind, mb, k],
            device_id={"tp": h * NX + peer_x(k)},
            device_id_type=MESH,
        ).wait_recv()

    def rs_copy(part, buf, kind, mb, k):
        rows = pl.ds(pl.multiple_of(peer_x(k) * C, C), C)
        return pltpu.make_async_remote_copy(
            src_ref=part.at[mb, rows],
            dst_ref=buf.at[mb, NX - k],
            send_sem=rs_send.at[kind, mb, k],
            recv_sem=rs_recv.at[kind, mb, NX - k],
            device_id={"tp": h * NX + peer_x(k)},
            device_id_type=MESH,
        )

    def rs_wait(part, buf, kind, mb, k):
        rows = pl.ds(pl.multiple_of(peer_x(k) * C, C), C)
        pltpu.make_async_remote_copy(
            src_ref=part.at[mb, rows],
            dst_ref=buf.at[mb, k],
            send_sem=rs_send.at[kind, mb, k],
            recv_sem=rs_recv.at[kind, mb, k],
            device_id={"tp": h * NX + peer_x(k)},
            device_id_type=MESH,
        ).wait_recv()

    def z_copy(src, buf, kind, mb, hh):
        to = s + 1 if kind == 0 else s - 1
        return pltpu.make_async_remote_copy(
            src_ref=src.at[mb],
            dst_ref=buf.at[mb, h],
            send_sem=z_send.at[kind, mb, hh],
            recv_sem=z_recv.at[kind, mb, h],
            device_id={"section": to % SECTIONS, "tp": hh * NX + x},
            device_id_type=MESH,
        )

    def z_wait(src, buf, kind, mb, hh):
        pltpu.make_async_remote_copy(
            src_ref=src.at[mb],
            dst_ref=buf.at[mb, hh],
            send_sem=z_send.at[kind, mb, hh],
            recv_sem=z_recv.at[kind, mb, hh],
            device_id={"tp": (1 - h) * NX + x},
            device_id_type=MESH,
        ).wait_recv()

    def zown_copy(src, buf, kind, mb):
        return pltpu.make_async_remote_copy(
            src_ref=src.at[mb],
            dst_ref=buf.at[mb],
            send_sem=z_send.at[kind, mb, 2],
            recv_sem=z_recv.at[kind, mb, 2],
            device_id={"tp": (1 - h) * NX + x},
            device_id_type=MESH,
        )

    def o_copy(ost, orecv, kind, mb, k):
        return pltpu.make_async_remote_copy(
            src_ref=ost.at[mb, peer_x(k)],
            dst_ref=orecv.at[mb, x],
            send_sem=o_send.at[kind, mb, k],
            recv_sem=o_recv.at[kind, mb, NX - k],
            device_id={"tp": h * NX + peer_x(k)},
            device_id_type=MESH,
        )

    def o_wait(ost, orecv, kind, mb, k):
        pltpu.make_async_remote_copy(
            src_ref=ost.at[mb, peer_x(k)],
            dst_ref=orecv.at[mb, peer_x(k)],
            send_sem=o_send.at[kind, mb, k],
            recv_sem=o_recv.at[kind, mb, k],
            device_id={"tp": h * NX + peer_x(k)},
            device_id_type=MESH,
        ).wait_recv()

    far_first = (2, 1, 3)

    def step_first(mb):
        @pl.when(s == 0)
        def _():
            xin[t] = acts[...]
            gather_blocks()
            for b in range(MB):
                xf, rms = rms_parts(full[b * R : (b + 1) * R])
                nb[b] = (xf / rms).astype(BF16)
                xrow[b] = full[pl.ds(pl.multiple_of(b * R + x * C, C), C), :]

        @pl.when(s == SECTIONS - 1)
        def _():
            xin[t] = cot[...]
            gather_blocks()
            for b in range(MB):
                dyb[b] = full[b * R : (b + 1) * R]
                dyrow[b] = full[pl.ds(pl.multiple_of(b * R + x * C, C), C), :]

    def head_fwd(mb):
        @pl.when(s > 0)
        def _():
            z_wait(zsend_f, zrecv_f, 0, mb, 0)
            z_wait(zsend_f, zrecv_f, 0, mb, 1)
            rows = (zrecv_f[mb, 0].astype(F32) + zrecv_f[mb, 1].astype(F32)).astype(BF16)
            xrow[mb] = rows
            xf, rms = rms_parts(rows)
            nb[mb, own] = (xf / rms).astype(BF16)
            for k in far_first:
                ag_copy(nb, 0, mb, k).start()

    def main_fwd(mb):
        @pl.when(s > 0)
        def _():
            for k in (1, 3, 2):
                ag_wait(nb, 0, mb, k)

        normed = nb[mb]
        gate = dot_nn(normed, wg[...]) * INV_D
        upper = dot_nn(normed, wu[...]) * INV_D
        sig = jax.nn.sigmoid(gate)
        active = gate * sig
        hidden = (active * upper).astype(BF16)
        part_f[mb] = (dot_nn(hidden, wd[...]) * INV_FF).astype(BF16)
        for k in far_first:
            rs_copy(part_f, rs_f, 0, mb, k).start()
        rows = pl.ds(pl.multiple_of(mb * R, R), R)
        out_hidden[rows, :] = hidden
        act_s[mb] = active
        slope_s[mb] = upper * sig * (1.0 + gate * (1.0 - sig))

    def half_sum(part, buf, kind, mb):
        for k in (1, 3, 2):
            rs_wait(part, buf, kind, mb, k)
        total = part[mb, own].astype(F32)
        for k in range(1, NX):
            total = total + buf[mb, k].astype(F32)
        return total

    def tail_fwd(mb):
        half = half_sum(part_f, rs_f, 0, mb)
        zsend_f[mb] = (half + 0.5 * xrow[mb].astype(F32)).astype(BF16)

        @pl.when(s < SECTIONS - 1)
        def _():
            z_copy(zsend_f, zrecv_f, 0, mb, 0).start()
            z_copy(zsend_f, zrecv_f, 0, mb, 1).start()

        zown_copy(zsend_f, zown_f, 0, mb).start()

    def head_bwd(mb):
        @pl.when(s < SECTIONS - 1)
        def _():
            z_wait(zsend_b, zrecv_b, 1, mb, 0)
            z_wait(zsend_b, zrecv_b, 1, mb, 1)
            rows = (zrecv_b[mb, 0].astype(F32) + zrecv_b[mb, 1].astype(F32)).astype(BF16)
            dyrow[mb] = rows
            dyb[mb, own] = rows
            for k in far_first:
                ag_copy(dyb, 1, mb, k).start()

    def main_bwd(mb):
        @pl.when(s < SECTIONS - 1)
        def _():
            for k in (1, 3, 2):
                ag_wait(dyb, 1, mb, k)

        dh = dot_nt(dyb[mb], wd[...]) * INV_FF
        dgate = (dh * slope_s[mb]).astype(BF16)
        dup = (dh * act_s[mb]).astype(BF16)
        part_b[mb] = ((dot_nt(dgate, wg[...]) + dot_nt(dup, wu[...])) * INV_D).astype(BF16)
        for k in far_first:
            rs_copy(part_b, rs_b, 1, mb, k).start()
        rows = pl.ds(pl.multiple_of(mb * R, R), R)
        out_dgate[rows, :] = dgate
        out_dup[rows, :] = dup

    def tail_bwd(mb):
        xf, rms = rms_parts(xrow[mb])
        normed = xf / rms
        half = half_sum(part_b, rs_b, 1, mb)
        stat = jnp.sum(half * normed, axis=1, keepdims=True) / D
        grad = 0.5 * dyrow[mb].astype(F32) + (half - normed * stat) / rms
        zsend_b[mb] = grad.astype(BF16)

        @pl.when(s > 0)
        def _():
            z_copy(zsend_b, zrecv_b, 1, mb, 0).start()
            z_copy(zsend_b, zrecv_b, 1, mb, 1).start()

        zown_copy(zsend_b, zown_b, 1, mb).start()

    def spread_columns(zsend, zown, ost, orecv, kind, mb):
        zown_copy(zsend, zown, kind, mb).wait_recv()
        rows = (zsend[mb].astype(F32) + zown[mb].astype(F32)).astype(BF16)
        wide = dot_nn(rows, spread[...]).astype(BF16)
        for q in range(NX):
            ost[mb, q] = wide[:, q * 128 : (q + 1) * 128]
        orecv[mb, x] = ost[mb, x]
        for k in far_first:
            o_copy(ost, orecv, kind, mb, k).start()

    def out_fwd(mb):
        @pl.when(mb == 0)
        def _():
            feature = lax.broadcasted_iota(jnp.int32, (D, NX * 128), 0) - h * (NX * BLOCK)
            place = lax.broadcasted_iota(jnp.int32, (D, NX * 128), 1)
            lane = place % 128
            hit = (feature == (place // 128) * BLOCK + lane) & (lane < BLOCK)
            spread[...] = jnp.where(hit, 1.0, 0.0).astype(BF16)

        spread_columns(zsend_f, zown_f, ost_f, orecv_f, 0, mb)

    def out_bwd(mb):
        spread_columns(zsend_b, zown_b, ost_b, orecv_b, 1, mb)

    def finish(mb):
        @pl.when(mb == 0)
        def _():
            for b in range(MB):
                out_nb[b * R : (b + 1) * R, :] = nb[b]
                out_dy[b * R : (b + 1) * R, :] = dyb[b]
                for kind, ost, orecv, out in ((0, ost_f, orecv_f, out_y), (1, ost_b, orecv_b, out_dx)):
                    for k in (1, 3, 2):
                        o_wait(ost, orecv, kind, b, k)
                    for j in range(NX):
                        rows = slice(b * R + j * C, b * R + (j + 1) * C)
                        out[rows, :] = orecv[b, j][:, :BLOCK]

    steps = {
        0: step_first,
        1: head_fwd,
        2: main_fwd,
        3: tail_fwd,
        4: head_bwd,
        5: main_bwd,
        6: tail_bwd,
        7: out_fwd,
        8: out_bwd,
        9: finish,
    }

    def run(index, carry):
        last = s == SECTIONS - 1
        code = jnp.int32(0)
        mb = jnp.int32(0)
        for place in range(len(EARLY)):
            here = index == place
            code = jnp.where(here, jnp.where(last, LAST[place][0], EARLY[place][0]), code)
            mb = jnp.where(here, jnp.where(last, LAST[place][1], EARLY[place][1]), mb)
        for number, step in steps.items():

            @pl.when(code == number)
            def _(step=step):
                step(mb)

        return carry

    lax.fori_loop(0, len(EARLY), run, 0)

    @pl.when(s == 0)
    def _():
        for k in order:
            in_copy(acts, k).wait_send()

    @pl.when(s == SECTIONS - 1)
    def _():
        for k in order:
            in_copy(cot, k).wait_send()

    def drain(mb, carry):
        for k in far_first:
            rs_copy(part_f, rs_f, 0, mb, k).wait_send()
            rs_copy(part_b, rs_b, 1, mb, k).wait_send()
            o_copy(ost_f, orecv_f, 0, mb, k).wait_send()
            o_copy(ost_b, orecv_b, 1, mb, k).wait_send()
        zown_copy(zsend_f, zown_f, 0, mb).wait_send()
        zown_copy(zsend_b, zown_b, 1, mb).wait_send()

        @pl.when(s > 0)
        def _():
            for k in far_first:
                ag_copy(nb, 0, mb, k).wait_send()
            for hh in range(2):
                z_copy(zsend_b, zrecv_b, 1, mb, hh).wait_send()

        @pl.when(s < SECTIONS - 1)
        def _():
            for k in far_first:
                ag_copy(dyb, 1, mb, k).wait_send()
            for hh in range(2):
                z_copy(zsend_f, zrecv_f, 0, mb, hh).wait_send()

        return carry

    lax.fori_loop(0, MB, drain, 0)


def chain(acts, cot, wg, wu, wd):
    hid = wg.shape[1]
    vm = pl.BlockSpec(memory_space=pltpu.VMEM)
    shape = jax.ShapeDtypeStruct
    dma = pltpu.SemaphoreType.DMA
    return pl.pallas_call(
        chain_kernel,
        out_shape=(
            shape((ROWS, BLOCK), BF16),
            shape((ROWS, BLOCK), BF16),
            shape((ROWS, D), BF16),
            shape((ROWS, hid), BF16),
            shape((ROWS, hid), BF16),
            shape((ROWS, hid), BF16),
            shape((ROWS, D), BF16),
        ),
        in_specs=[vm] * 5,
        out_specs=[vm] * 7,
        scratch_shapes=[
            pltpu.VMEM((TP, ROWS, BLOCK), BF16),
            pltpu.VMEM((ROWS, D), BF16),
            pltpu.VMEM((MB, R, hid), F32),
            pltpu.VMEM((MB, R, hid), F32),
            pltpu.VMEM((D, NX * 128), BF16),
            pltpu.VMEM((MB, R, D), BF16),
            pltpu.VMEM((MB, R, D), BF16),
            pltpu.VMEM((MB, C, D), BF16),
            pltpu.VMEM((MB, C, D), BF16),
            pltpu.VMEM((MB, R, D), BF16),
            pltpu.VMEM((MB, R, D), BF16),
            pltpu.VMEM((MB, NX, C, D), BF16),
            pltpu.VMEM((MB, NX, C, D), BF16),
            pltpu.VMEM((MB, C, D), BF16),
            pltpu.VMEM((MB, C, D), BF16),
            pltpu.VMEM((MB, 2, C, D), BF16),
            pltpu.VMEM((MB, 2, C, D), BF16),
            pltpu.VMEM((MB, C, D), BF16),
            pltpu.VMEM((MB, C, D), BF16),
            pltpu.VMEM((MB, NX, C, 128), BF16),
            pltpu.VMEM((MB, NX, C, 128), BF16),
            pltpu.VMEM((MB, NX, C, 128), BF16),
            pltpu.VMEM((MB, NX, C, 128), BF16),
            dma((TP,)),
            dma((TP,)),
            dma((2, MB, NX)),
            dma((2, MB, NX)),
            dma((2, MB, NX)),
            dma((2, MB, NX)),
            dma((2, MB, 3)),
            dma((2, MB, 3)),
            dma((2, MB, NX)),
            dma((2, MB, NX)),
        ],
        compiler_params=pltpu.CompilerParams(
            collective_id=0, has_side_effects=True, vmem_limit_bytes=48 * 1024 * 1024
        ),
        name="chain",
    )(acts, cot, wg, wu, wd)


def contract_rows(left, right):
    return lax.dot_general(left, right, (((0,), (0,)), ((), ())), preferred_element_type=F32)


def adam_step(weight, first, second, grad):
    m_new = BETA_ONE * first.astype(F32) + (1.0 - BETA_ONE) * grad
    v_new = BETA_TWO * second.astype(F32) + (1.0 - BETA_TWO) * grad * grad
    return (weight.astype(F32) - LEARN * m_new / (jnp.sqrt(v_new) + ADAM_EPS)).astype(BF16)


def gossip(*updated, distance):
    peers = lax.axis_size("rep")
    pairs = [(i, (i + distance) % peers) for i in range(peers)]
    return tuple(
        ((own.astype(F32) + lax.ppermute(own, "rep", pairs).astype(F32)) * 0.5).astype(BF16)
        for own in updated
    )


def on_device(
    acts, cotangent, w_gate, w_up, w_down, m_gate, m_up, m_down, v_gate, v_up, v_down, steps
):
    wg, wu, wd = w_gate[0, 0], w_up[0, 0], w_down[0, 0]
    y, dx, nb, hidden, dgate, dup, dy = chain(acts[0], cotangent[0], wg, wu, wd)
    new_down = adam_step(wd, m_down[0, 0], v_down[0, 0], contract_rows(hidden, dy) * INV_FF)
    new_gate = adam_step(wg, m_gate[0, 0], v_gate[0, 0], contract_rows(nb, dgate) * INV_D)
    new_up = adam_step(wu, m_up[0, 0], v_up[0, 0], contract_rows(nb, dup) * INV_D)
    levels = lax.axis_size("rep").bit_length() - 1
    branches = [functools.partial(gossip, distance=2**level) for level in range(levels)]
    new_down, new_gate, new_up = lax.switch(
        steps[0] % levels, branches, new_down, new_gate, new_up
    )
    return (
        y[None, None],
        dx[None, None],
        new_gate[None, None],
        new_up[None, None],
        new_down[None, None],
    )


def solution(mesh):
    return jax.shard_map(
        on_device,
        mesh=mesh,
        in_specs=(
            P("rep", None, "tp"),
            P("rep", None, "tp"),
            P("section", "rep", None, "tp"),
            P("section", "rep", None, "tp"),
            P("section", "rep", "tp", None),
            P("section", "rep", None, "tp"),
            P("section", "rep", None, "tp"),
            P("section", "rep", "tp", None),
            P("section", "rep", None, "tp"),
            P("section", "rep", None, "tp"),
            P("section", "rep", "tp", None),
            P("section"),
        ),
        out_specs=(
            P("section", "rep", None, "tp"),
            P("section", "rep", None, "tp"),
            P("section", "rep", None, "tp"),
            P("section", "rep", None, "tp"),
            P("section", "rep", "tp", None),
        ),
        check_vma=False,
    )
```

```python
import functools
import math

import jax
import jax.numpy as jnp
from jax import lax
from jax.experimental import pallas as pl
from jax.experimental.pallas import tpu as pltpu
from jax.sharding import PartitionSpec as P

D = 896
FF = 4864
ROWS = 256
SECTIONS = 4
TP = 8
NX = 4
BLOCK = D // TP
MB = 4
R = ROWS // MB
C = R // NX

NORM_EPS = 1e-06
ADAM_EPS = 1e-08
LEARN = 0.3
BETA_ONE = 0.9
BETA_TWO = 0.95
INV_D = 1.0 / math.sqrt(D)
INV_FF = 1.0 / math.sqrt(FF)
MESH = pl.DeviceIdType.MESH
BF16 = jnp.bfloat16
F32 = jnp.float32

CODES = {name: number for number, name in enumerate("IHMThmtOoDGUE-")}


def plan(text):
    return [(CODES[name], int(mb)) for name, mb in zip(text[::2], text[1::2])]


FORWARD = "I0H0H1M0H2M1H3T0M2T1M3T2T3O0O1O2O3"
BACKWARD = "h0h1m0h2m1h3t0m2t1m3t2"
FIRST = plan(FORWARD + BACKWARD + "D0t3G0U0o0o1o2o3E0")
MIDDLE = plan(FORWARD + BACKWARD + "t3D0G0U0o0o1o2o3E0")
TURN = plan("I0H0H1M0m0H2M1m1t0H3M2m2t1M3m3t2t3")
LAST = TURN + plan("D0G0U0T0T1T2T3O0O1O2O3o0o1o2o3E0")
LAST = LAST + plan("-0") * (len(MIDDLE) - len(LAST))


def rms_parts(rows):
    xf = rows.astype(F32)
    rms = jnp.sqrt(jnp.mean(xf * xf, axis=1, keepdims=True) + NORM_EPS)
    return xf, rms


def dot_nn(left, right):
    return lax.dot_general(left, right, (((1,), (0,)), ((), ())), preferred_element_type=F32)


def dot_tn(left, right):
    return lax.dot_general(left, right, (((0,), (0,)), ((), ())), preferred_element_type=F32)


def dot_nt(left, right):
    return lax.dot_general(left, right, (((1,), (1,)), ((), ())), preferred_element_type=F32)


def chain_kernel(
    acts,
    cot,
    wg_hbm,
    wu_hbm,
    wd_hbm,
    mg_hbm,
    mu_hbm,
    md_hbm,
    vg_hbm,
    vu_hbm,
    vd_hbm,
    out_y,
    out_dx,
    out_gate,
    out_up,
    out_down,
    wg,
    wu,
    wd,
    mg,
    mu,
    md,
    vg,
    vu,
    vd,
    ng,
    nu,
    nd,
    grad,
    xin,
    full,
    hidden_s,
    dgate_s,
    dup_s,
    act_s,
    slope_s,
    spread,
    nb,
    dyb,
    xrow,
    dyrow,
    part_f,
    part_b,
    rs_f,
    rs_b,
    zsend_f,
    zsend_b,
    zrecv_f,
    zrecv_b,
    zown_f,
    zown_b,
    ost_f,
    ost_b,
    orecv_f,
    orecv_b,
    load_sem,
    store_sem,
    in_send,
    in_recv,
    ag_send,
    ag_recv,
    rs_send,
    rs_recv,
    z_send,
    z_recv,
    o_send,
    o_recv,
):
    s = lax.axis_index("section")
    t = lax.axis_index("tp")
    h = t // NX
    x = t % NX
    own = pl.ds(pl.multiple_of(x * C, C), C)

    def at_tp(where):
        return {"tp": where}

    def peer_x(k):
        return (x + k) % NX

    loads = [
        pltpu.make_async_copy(src, dst, load_sem.at[number])
        for number, (src, dst) in enumerate(
            (
                (wg_hbm, wg),
                (wu_hbm, wu),
                (wd_hbm, wd),
                (md_hbm, md),
                (vd_hbm, vd),
                (mg_hbm, mg),
                (vg_hbm, vg),
                (mu_hbm, mu),
                (vu_hbm, vu),
            )
        )
    ]
    stores = [
        pltpu.make_async_copy(src, dst, store_sem.at[number])
        for number, (src, dst) in enumerate(((nd, out_down), (ng, out_gate), (nu, out_up)))
    ]
    for load in loads[:3]:
        load.start()

    barrier = pltpu.get_barrier_semaphore()
    for k in range(1, TP):
        pl.semaphore_signal(barrier, inc=1, device_id={"tp": (t + k) % TP}, device_id_type=MESH)
    for step in (1, SECTIONS - 1):
        for hh in range(2):
            pl.semaphore_signal(
                barrier,
                inc=1,
                device_id={"section": (s + step) % SECTIONS, "tp": hh * NX + x},
                device_id_type=MESH,
            )
    pl.semaphore_wait(barrier, TP - 1 + 4)

    def block_of(who):
        return pl.ds(pl.multiple_of(who * BLOCK, BLOCK), BLOCK)

    def in_copy(src, k):
        return pltpu.make_async_remote_copy(
            src_ref=src,
            dst_ref=xin.at[block_of(t)],
            send_sem=in_send.at[k],
            recv_sem=in_recv.at[t],
            device_id={"tp": (t + k) % TP},
            device_id_type=MESH,
        )

    def in_wait(k):
        who = (t + k) % TP
        pltpu.make_async_remote_copy(
            src_ref=xin.at[block_of(who)],
            dst_ref=xin.at[block_of(who)],
            send_sem=in_send.at[0],
            recv_sem=in_recv.at[who],
            device_id={"tp": who},
            device_id_type=MESH,
        ).wait_recv()

    order = (4, 5, 3, 6, 2, 7, 1)

    @pl.when(s == 0)
    def _():
        for k in order:
            in_copy(acts, k).start()

    @pl.when(s == SECTIONS - 1)
    def _():
        for k in order:
            in_copy(cot, k).start()

    for load in loads[3:]:
        load.start()

    def gather_blocks():
        for k in range(1, TP):
            in_wait(k)
        full[...] = xin[...].astype(F32).T.astype(BF16)

    def ag_copy(buf, kind, mb, k):
        return pltpu.make_async_remote_copy(
            src_ref=buf.at[mb, own],
            dst_ref=buf.at[mb, own],
            send_sem=ag_send.at[kind, mb, k],
            recv_sem=ag_recv.at[kind, mb, NX - k],
            device_id={"tp": h * NX + peer_x(k)},
            device_id_type=MESH,
        )

    def ag_wait(buf, kind, mb, k):
        rows = pl.ds(pl.multiple_of(peer_x(k) * C, C), C)
        pltpu.make_async_remote_copy(
            src_ref=buf.at[mb, rows],
            dst_ref=buf.at[mb, rows],
            send_sem=ag_send.at[kind, mb, k],
            recv_sem=ag_recv.at[kind, mb, k],
            device_id={"tp": h * NX + peer_x(k)},
            device_id_type=MESH,
        ).wait_recv()

    def rs_copy(part, buf, kind, mb, k):
        rows = pl.ds(pl.multiple_of(peer_x(k) * C, C), C)
        return pltpu.make_async_remote_copy(
            src_ref=part.at[mb, rows],
            dst_ref=buf.at[mb, NX - k],
            send_sem=rs_send.at[kind, mb, k],
            recv_sem=rs_recv.at[kind, mb, NX - k],
            device_id={"tp": h * NX + peer_x(k)},
            device_id_type=MESH,
        )

    def rs_wait(part, buf, kind, mb, k):
        rows = pl.ds(pl.multiple_of(peer_x(k) * C, C), C)
        pltpu.make_async_remote_copy(
            src_ref=part.at[mb, rows],
            dst_ref=buf.at[mb, k],
            send_sem=rs_send.at[kind, mb, k],
            recv_sem=rs_recv.at[kind, mb, k],
            device_id={"tp": h * NX + peer_x(k)},
            device_id_type=MESH,
        ).wait_recv()

    def z_copy(src, buf, kind, mb, hh):
        to = s + 1 if kind == 0 else s - 1
        return pltpu.make_async_remote_copy(
            src_ref=src.at[mb],
            dst_ref=buf.at[mb, h],
            send_sem=z_send.at[kind, mb, hh],
            recv_sem=z_recv.at[kind, mb, h],
            device_id={"section": to % SECTIONS, "tp": hh * NX + x},
            device_id_type=MESH,
        )

    def z_wait(src, buf, kind, mb, hh):
        pltpu.make_async_remote_copy(
            src_ref=src.at[mb],
            dst_ref=buf.at[mb, hh],
            send_sem=z_send.at[kind, mb, hh],
            recv_sem=z_recv.at[kind, mb, hh],
            device_id={"tp": (1 - h) * NX + x},
            device_id_type=MESH,
        ).wait_recv()

    def zown_copy(src, buf, kind, mb):
        return pltpu.make_async_remote_copy(
            src_ref=src.at[mb],
            dst_ref=buf.at[mb],
            send_sem=z_send.at[kind, mb, 2],
            recv_sem=z_recv.at[kind, mb, 2],
            device_id={"tp": (1 - h) * NX + x},
            device_id_type=MESH,
        )

    def o_copy(ost, orecv, kind, mb, k):
        return pltpu.make_async_remote_copy(
            src_ref=ost.at[mb, peer_x(k)],
            dst_ref=orecv.at[mb, x],
            send_sem=o_send.at[kind, mb, k],
            recv_sem=o_recv.at[kind, mb, NX - k],
            device_id={"tp": h * NX + peer_x(k)},
            device_id_type=MESH,
        )

    def o_wait(ost, orecv, kind, mb, k):
        pltpu.make_async_remote_copy(
            src_ref=ost.at[mb, peer_x(k)],
            dst_ref=orecv.at[mb, peer_x(k)],
            send_sem=o_send.at[kind, mb, k],
            recv_sem=o_recv.at[kind, mb, k],
            device_id={"tp": h * NX + peer_x(k)},
            device_id_type=MESH,
        ).wait_recv()

    far_first = (2, 1, 3)

    def step_first(mb):
        for load in loads[:3]:
            load.wait()

        @pl.when(s == 0)
        def _():
            xin[block_of(t), :] = acts[...]
            gather_blocks()
            for b in range(MB):
                xf, rms = rms_parts(full[b * R : (b + 1) * R, :])
                nb[b] = (xf / rms).astype(BF16)
                xrow[b] = full[pl.ds(pl.multiple_of(b * R + x * C, C), C), :]

        @pl.when(s == SECTIONS - 1)
        def _():
            xin[block_of(t), :] = cot[...]
            gather_blocks()
            for b in range(MB):
                dyb[b] = full[b * R : (b + 1) * R, :]
                dyrow[b] = full[pl.ds(pl.multiple_of(b * R + x * C, C), C), :]

    def head_fwd(mb):
        @pl.when(s > 0)
        def _():
            z_wait(zsend_f, zrecv_f, 0, mb, 0)
            z_wait(zsend_f, zrecv_f, 0, mb, 1)
            rows = (zrecv_f[mb, 0].astype(F32) + zrecv_f[mb, 1].astype(F32)).astype(BF16)
            xrow[mb] = rows
            xf, rms = rms_parts(rows)
            nb[mb, own] = (xf / rms).astype(BF16)
            for k in far_first:
                ag_copy(nb, 0, mb, k).start()

    def main_fwd(mb):
        @pl.when(s > 0)
        def _():
            for k in (1, 3, 2):
                ag_wait(nb, 0, mb, k)

        normed = nb[mb]
        gate = dot_nt(normed, wg[...]) * INV_D
        upper = dot_nt(normed, wu[...]) * INV_D
        sig = jax.nn.sigmoid(gate)
        active = gate * sig
        hidden = (active * upper).astype(BF16)
        part_f[mb] = (dot_nn(hidden, wd[...]) * INV_FF).astype(BF16)
        for k in far_first:
            rs_copy(part_f, rs_f, 0, mb, k).start()
        hidden_s[mb] = hidden
        act_s[mb] = active
        slope_s[mb] = upper * sig * (1.0 + gate * (1.0 - sig))

    def half_sum(part, buf, kind, mb):
        for k in (1, 3, 2):
            rs_wait(part, buf, kind, mb, k)
        total = part[mb, own].astype(F32)
        for k in range(1, NX):
            total = total + buf[mb, k].astype(F32)
        return total

    def tail_fwd(mb):
        half = half_sum(part_f, rs_f, 0, mb)
        zsend_f[mb] = (half + 0.5 * xrow[mb].astype(F32)).astype(BF16)

        @pl.when(s < SECTIONS - 1)
        def _():
            z_copy(zsend_f, zrecv_f, 0, mb, 0).start()
            z_copy(zsend_f, zrecv_f, 0, mb, 1).start()

        zown_copy(zsend_f, zown_f, 0, mb).start()

    def head_bwd(mb):
        @pl.when(s < SECTIONS - 1)
        def _():
            z_wait(zsend_b, zrecv_b, 1, mb, 0)
            z_wait(zsend_b, zrecv_b, 1, mb, 1)
            rows = (zrecv_b[mb, 0].astype(F32) + zrecv_b[mb, 1].astype(F32)).astype(BF16)
            dyrow[mb] = rows
            dyb[mb, own] = rows
            for k in far_first:
                ag_copy(dyb, 1, mb, k).start()

    def main_bwd(mb):
        @pl.when(s < SECTIONS - 1)
        def _():
            for k in (1, 3, 2):
                ag_wait(dyb, 1, mb, k)

        dh = dot_nt(dyb[mb], wd[...]) * INV_FF
        dgate = (dh * slope_s[mb]).astype(BF16)
        dup = (dh * act_s[mb]).astype(BF16)
        part_b[mb] = ((dot_nn(dgate, wg[...]) + dot_nn(dup, wu[...])) * INV_D).astype(BF16)
        for k in far_first:
            rs_copy(part_b, rs_b, 1, mb, k).start()
        dgate_s[mb] = dgate
        dup_s[mb] = dup

    def tail_bwd(mb):
        xf, rms = rms_parts(xrow[mb])
        normed = xf / rms
        half = half_sum(part_b, rs_b, 1, mb)
        stat = jnp.sum(half * normed, axis=1, keepdims=True) / D
        grad = 0.5 * dyrow[mb].astype(F32) + (half - normed * stat) / rms
        zsend_b[mb] = grad.astype(BF16)

        @pl.when(s > 0)
        def _():
            z_copy(zsend_b, zrecv_b, 1, mb, 0).start()
            z_copy(zsend_b, zrecv_b, 1, mb, 1).start()

        zown_copy(zsend_b, zown_b, 1, mb).start()

    def spread_columns(zsend, zown, ost, orecv, kind, mb):
        zown_copy(zsend, zown, kind, mb).wait_recv()
        rows = (zsend[mb].astype(F32) + zown[mb].astype(F32)).astype(BF16)
        wide = dot_nn(rows, spread[...]).astype(BF16)
        for q in range(NX):
            ost[mb, q] = wide[:, q * 128 : (q + 1) * 128]
        orecv[mb, x] = ost[mb, x]
        for k in far_first:
            o_copy(ost, orecv, kind, mb, k).start()

    def out_fwd(mb):
        @pl.when(mb == 0)
        def _():
            feature = lax.broadcasted_iota(jnp.int32, (D, NX * 128), 0) - h * (NX * BLOCK)
            place = lax.broadcasted_iota(jnp.int32, (D, NX * 128), 1)
            lane = place % 128
            hit = (feature == (place // 128) * BLOCK + lane) & (lane < BLOCK)
            spread[...] = jnp.where(hit, 1.0, 0.0).astype(BF16)

        spread_columns(zsend_f, zown_f, ost_f, orecv_f, 0, mb)

    def out_bwd(mb):
        spread_columns(zsend_b, zown_b, ost_b, orecv_b, 1, mb)

    def update(number, units, rows, scale, weight, first, second, new):
        loads[3 + 2 * number].wait()
        loads[4 + 2 * number].wait()
        hid = weight.shape[0]
        grad[...] = dot_tn(units[...].reshape(ROWS, hid), rows[...].reshape(ROWS, D)) * scale

        def piece(index, carry):
            part = pl.ds(pl.multiple_of(index * 32, 32), 32)
            g = grad[part, :]
            m_new = BETA_ONE * first[part, :].astype(F32) + (1.0 - BETA_ONE) * g
            v_new = BETA_TWO * second[part, :].astype(F32) + (1.0 - BETA_TWO) * g * g
            step = LEARN * m_new / (jnp.sqrt(v_new) + ADAM_EPS)
            new[part, :] = (weight[part, :].astype(F32) - step).astype(BF16)
            return carry

        lax.fori_loop(0, hid // 32, piece, 0)
        stores[number].start()

    def update_down(mb):
        update(0, hidden_s, dyb, INV_FF, wd, md, vd, nd)

    def update_gate(mb):
        update(1, dgate_s, nb, INV_D, wg, mg, vg, ng)

    def update_up(mb):
        update(2, dup_s, nb, INV_D, wu, mu, vu, nu)

    def finish(mb):
        for kind, ost, orecv, out in ((0, ost_f, orecv_f, out_y), (1, ost_b, orecv_b, out_dx)):
            for b in range(MB):
                for k in (1, 3, 2):
                    o_wait(ost, orecv, kind, b, k)
            out[...] = orecv[...].reshape(ROWS, 128).astype(F32).T[:BLOCK].astype(BF16)

    steps = (
        step_first,
        head_fwd,
        main_fwd,
        tail_fwd,
        head_bwd,
        main_bwd,
        tail_bwd,
        out_fwd,
        out_bwd,
        update_down,
        update_gate,
        update_up,
        finish,
    )

    def run(index, carry):
        code = jnp.int32(0)
        mb = jnp.int32(0)
        for place, (first, middle, last) in enumerate(zip(FIRST, MIDDLE, LAST)):
            here = index == place
            for field in range(2):
                value = jnp.where(s == SECTIONS - 1, last[field], middle[field])
                value = jnp.where(s == 0, first[field], value)
                if field == 0:
                    code = jnp.where(here, value, code)
                else:
                    mb = jnp.where(here, value, mb)
        for number, step in enumerate(steps):

            @pl.when(code == number)
            def _(step=step):
                step(mb)

        return carry

    lax.fori_loop(0, len(MIDDLE), run, 0)

    for store in stores:
        store.wait()

    @pl.when(s == 0)
    def _():
        for k in order:
            in_copy(acts, k).wait_send()

    @pl.when(s == SECTIONS - 1)
    def _():
        for k in order:
            in_copy(cot, k).wait_send()

    def drain(mb, carry):
        for k in far_first:
            rs_copy(part_f, rs_f, 0, mb, k).wait_send()
            rs_copy(part_b, rs_b, 1, mb, k).wait_send()
            o_copy(ost_f, orecv_f, 0, mb, k).wait_send()
            o_copy(ost_b, orecv_b, 1, mb, k).wait_send()
        zown_copy(zsend_f, zown_f, 0, mb).wait_send()
        zown_copy(zsend_b, zown_b, 1, mb).wait_send()

        @pl.when(s > 0)
        def _():
            for k in far_first:
                ag_copy(nb, 0, mb, k).wait_send()
            for hh in range(2):
                z_copy(zsend_b, zrecv_b, 1, mb, hh).wait_send()

        @pl.when(s < SECTIONS - 1)
        def _():
            for k in far_first:
                ag_copy(dyb, 1, mb, k).wait_send()
            for hh in range(2):
                z_copy(zsend_f, zrecv_f, 0, mb, hh).wait_send()

        return carry

    lax.fori_loop(0, MB, drain, 0)


def chain(acts, cot, weights, firsts, seconds):
    hid = weights[0].shape[0]
    vm = pl.BlockSpec(memory_space=pltpu.VMEM)
    hbm = pl.BlockSpec(memory_space=pl.ANY)
    shape = jax.ShapeDtypeStruct
    dma = pltpu.SemaphoreType.DMA
    return pl.pallas_call(
        chain_kernel,
        out_shape=(shape((BLOCK, ROWS), BF16),) * 2 + (shape((hid, D), BF16),) * 3,
        in_specs=[vm] * 2 + [hbm] * 9,
        out_specs=[vm] * 2 + [hbm] * 3,
        scratch_shapes=[pltpu.VMEM((hid, D), BF16)] * 12
        + [
            pltpu.VMEM((hid, D), F32),
            pltpu.VMEM((D, ROWS), BF16),
            pltpu.VMEM((ROWS, D), BF16),
            pltpu.VMEM((MB, R, hid), BF16),
            pltpu.VMEM((MB, R, hid), BF16),
            pltpu.VMEM((MB, R, hid), BF16),
            pltpu.VMEM((MB, R, hid), F32),
            pltpu.VMEM((MB, R, hid), F32),
            pltpu.VMEM((D, NX * 128), BF16),
            pltpu.VMEM((MB, R, D), BF16),
            pltpu.VMEM((MB, R, D), BF16),
            pltpu.VMEM((MB, C, D), BF16),
            pltpu.VMEM((MB, C, D), BF16),
            pltpu.VMEM((MB, R, D), BF16),
            pltpu.VMEM((MB, R, D), BF16),
            pltpu.VMEM((MB, NX, C, D), BF16),
            pltpu.VMEM((MB, NX, C, D), BF16),
            pltpu.VMEM((MB, C, D), BF16),
            pltpu.VMEM((MB, C, D), BF16),
            pltpu.VMEM((MB, 2, C, D), BF16),
            pltpu.VMEM((MB, 2, C, D), BF16),
            pltpu.VMEM((MB, C, D), BF16),
            pltpu.VMEM((MB, C, D), BF16),
            pltpu.VMEM((MB, NX, C, 128), BF16),
            pltpu.VMEM((MB, NX, C, 128), BF16),
            pltpu.VMEM((MB, NX, C, 128), BF16),
            pltpu.VMEM((MB, NX, C, 128), BF16),
            dma((9,)),
            dma((3,)),
            dma((TP,)),
            dma((TP,)),
            dma((2, MB, NX)),
            dma((2, MB, NX)),
            dma((2, MB, NX)),
            dma((2, MB, NX)),
            dma((2, MB, 3)),
            dma((2, MB, 3)),
            dma((2, MB, NX)),
            dma((2, MB, NX)),
        ],
        compiler_params=pltpu.CompilerParams(
            collective_id=0, has_side_effects=True, vmem_limit_bytes=56 * 1024 * 1024
        ),
        name="chain",
    )(acts, cot, *weights, *firsts, *seconds)


def gossip(*updated, distance):
    peers = lax.axis_size("rep")
    pairs = [(i, (i + distance) % peers) for i in range(peers)]
    return tuple(lax.ppermute(own, "rep", pairs) for own in updated)


def mean(own, other):
    return ((own.astype(F32) + other.astype(F32)) * 0.5).astype(BF16)


def on_device(
    acts, cotangent, w_gate, w_up, w_down, m_gate, m_up, m_down, v_gate, v_up, v_down, steps
):
    def by_units(gate, up, down):
        return gate[0, 0].T, up[0, 0].T, down[0, 0]

    y, dx, *updated = chain(
        acts[0].T,
        cotangent[0].T,
        by_units(w_gate, w_up, w_down),
        by_units(m_gate, m_up, m_down),
        by_units(v_gate, v_up, v_down),
    )
    levels = lax.axis_size("rep").bit_length() - 1
    branches = [functools.partial(gossip, distance=2**level) for level in range(levels)]
    others = lax.switch(steps[0] % levels, branches, *updated)
    new_gate, new_up, new_down = (mean(own, other) for own, other in zip(updated, others))
    return (
        y.T[None, None],
        dx.T[None, None],
        new_gate.T[None, None],
        new_up.T[None, None],
        new_down[None, None],
    )


def solution(mesh):
    return jax.shard_map(
        on_device,
        mesh=mesh,
        in_specs=(
            P("rep", None, "tp"),
            P("rep", None, "tp"),
            P("section", "rep", None, "tp"),
            P("section", "rep", None, "tp"),
            P("section", "rep", "tp", None),
            P("section", "rep", None, "tp"),
            P("section", "rep", None, "tp"),
            P("section", "rep", "tp", None),
            P("section", "rep", None, "tp"),
            P("section", "rep", None, "tp"),
            P("section", "rep", "tp", None),
            P("section"),
        ),
        out_specs=(
            P("section", "rep", None, "tp"),
            P("section", "rep", None, "tp"),
            P("section", "rep", None, "tp"),
            P("section", "rep", None, "tp"),
            P("section", "rep", "tp", None),
        ),
        check_vma=False,
    )
```

```python
import functools
import math

import jax
import jax.numpy as jnp
from jax import lax
from jax.experimental import pallas as pl
from jax.experimental.pallas import tpu as pltpu
from jax.sharding import PartitionSpec as P

D = 896
FF = 4864
ROWS = 256
SECTIONS = 4
TP = 8
NX = 4
BLOCK = D // TP
MB = 4
R = ROWS // MB
HALF = ROWS // 2
C = R // NX

NORM_EPS = 1e-06
ADAM_EPS = 1e-08
LEARN = 0.3
BETA_ONE = 0.9
BETA_TWO = 0.95
INV_D = 1.0 / math.sqrt(D)
INV_FF = 1.0 / math.sqrt(FF)
MESH = pl.DeviceIdType.MESH
BF16 = jnp.bfloat16
F32 = jnp.float32

CODES = {name: number for number, name in enumerate("IHMThmtOoDGUE-")}


def plan(text):
    return [(CODES[name], int(mb)) for name, mb in zip(text[::2], text[1::2])]


START = "I0H0H1M0I1H2M1H3T0M2T1M3T2T3"
RETURN = "O0O1O2O3h0h1m0h2m1h3t0m2t1m3t2"
FIRST = plan(START + RETURN + "o0o1D0t3o2o3G0U0E0")
MIDDLE = plan(START + RETURN + "t3o0o1o2o3D0G0U0E0")
TURN = plan("I0I1H0H1M0m0H2M1m1t0H3M2m2t1M3m3t2t3")
LAST = TURN + plan("D0G0U0T0T1T2T3O0O1O2O3o0o1o2o3E0")
LAST = LAST + plan("-0") * (len(MIDDLE) - len(LAST))


def rms_parts(rows):
    xf = rows.astype(F32)
    rms = jnp.sqrt(jnp.mean(xf * xf, axis=1, keepdims=True) + NORM_EPS)
    return xf, rms


def dot_nn(left, right):
    return lax.dot_general(left, right, (((1,), (0,)), ((), ())), preferred_element_type=F32)


def dot_tn(left, right):
    return lax.dot_general(left, right, (((0,), (0,)), ((), ())), preferred_element_type=F32)


def dot_nt(left, right):
    return lax.dot_general(left, right, (((1,), (1,)), ((), ())), preferred_element_type=F32)


def chain_kernel(
    acts,
    cot,
    wg_hbm,
    wu_hbm,
    wd_hbm,
    mg_hbm,
    mu_hbm,
    md_hbm,
    vg_hbm,
    vu_hbm,
    vd_hbm,
    out_y,
    out_dx,
    out_gate,
    out_up,
    out_down,
    wg,
    wu,
    wd,
    mg,
    mu,
    md,
    vg,
    vu,
    vd,
    ng,
    nu,
    nd,
    grad,
    xin,
    full,
    hidden_s,
    dgate_s,
    dup_s,
    act_s,
    slope_s,
    spread,
    nb,
    dyb,
    xrow,
    dyrow,
    part_f,
    part_b,
    rs_f,
    rs_b,
    zsend_f,
    zsend_b,
    zrecv_f,
    zrecv_b,
    ost_f,
    ost_b,
    orecv_f,
    orecv_b,
    load_sem,
    store_sem,
    in_send,
    in_recv,
    ag_send,
    ag_recv,
    rs_send,
    rs_recv,
    z_send,
    z_recv,
    o_send,
    o_recv,
):
    s = lax.axis_index("section")
    t = lax.axis_index("tp")
    h = t // NX
    x = t % NX
    own = pl.ds(pl.multiple_of(x * C, C), C)

    def at_tp(where):
        return {"tp": where}

    def peer_x(k):
        return (x + k) % NX

    loads = [
        pltpu.make_async_copy(src, dst, load_sem.at[number])
        for number, (src, dst) in enumerate(
            (
                (wg_hbm, wg),
                (wu_hbm, wu),
                (wd_hbm, wd),
                (md_hbm, md),
                (vd_hbm, vd),
                (mg_hbm, mg),
                (vg_hbm, vg),
                (mu_hbm, mu),
                (vu_hbm, vu),
            )
        )
    ]
    stores = [
        pltpu.make_async_copy(src, dst, store_sem.at[number])
        for number, (src, dst) in enumerate(((nd, out_down), (ng, out_gate), (nu, out_up)))
    ]
    for load in loads[:3]:
        load.start()

    barrier = pltpu.get_barrier_semaphore()
    for k in range(1, TP):
        pl.semaphore_signal(barrier, inc=1, device_id={"tp": (t + k) % TP}, device_id_type=MESH)
    for step in (1, SECTIONS - 1):
        for hh in range(2):
            pl.semaphore_signal(
                barrier,
                inc=1,
                device_id={"section": (s + step) % SECTIONS, "tp": hh * NX + x},
                device_id_type=MESH,
            )
    pl.semaphore_wait(barrier, TP - 1 + 4)

    def block_of(who):
        return pl.ds(pl.multiple_of(who * BLOCK, BLOCK), BLOCK)

    def half_of(piece):
        return pl.ds(pl.multiple_of(piece * HALF, HALF), HALF)

    def in_copy(src, piece, k):
        return pltpu.make_async_remote_copy(
            src_ref=src.at[:, half_of(piece)],
            dst_ref=xin.at[block_of(t), half_of(piece)],
            send_sem=in_send.at[piece, k],
            recv_sem=in_recv.at[piece, t],
            device_id={"tp": (t + k) % TP},
            device_id_type=MESH,
        )

    def in_wait(piece, k):
        who = (t + k) % TP
        pltpu.make_async_remote_copy(
            src_ref=xin.at[block_of(who), half_of(piece)],
            dst_ref=xin.at[block_of(who), half_of(piece)],
            send_sem=in_send.at[piece, k],
            recv_sem=in_recv.at[piece, who],
            device_id={"tp": who},
            device_id_type=MESH,
        ).wait_recv()

    order = (4, 5, 3, 6, 2, 7, 1)

    @pl.when(s == 0)
    def _():
        for piece in range(2):
            for k in order:
                in_copy(acts, piece, k).start()

    @pl.when(s == SECTIONS - 1)
    def _():
        for piece in range(2):
            for k in order:
                in_copy(cot, piece, k).start()

    for load in loads[3:]:
        load.start()

    def gather_blocks(src, piece):
        xin[block_of(t), half_of(piece)] = src[:, half_of(piece)]
        for k in range(1, TP):
            in_wait(piece, k)
        full[half_of(piece), :] = xin[:, half_of(piece)].astype(F32).T.astype(BF16)

    def ag_copy(buf, kind, mb, k):
        return pltpu.make_async_remote_copy(
            src_ref=buf.at[mb, own],
            dst_ref=buf.at[mb, own],
            send_sem=ag_send.at[kind, mb, k],
            recv_sem=ag_recv.at[kind, mb, NX - k],
            device_id={"tp": h * NX + peer_x(k)},
            device_id_type=MESH,
        )

    def ag_wait(buf, kind, mb, k):
        rows = pl.ds(pl.multiple_of(peer_x(k) * C, C), C)
        pltpu.make_async_remote_copy(
            src_ref=buf.at[mb, rows],
            dst_ref=buf.at[mb, rows],
            send_sem=ag_send.at[kind, mb, k],
            recv_sem=ag_recv.at[kind, mb, k],
            device_id={"tp": h * NX + peer_x(k)},
            device_id_type=MESH,
        ).wait_recv()

    def rs_copy(part, buf, kind, mb, k):
        rows = pl.ds(pl.multiple_of(peer_x(k) * C, C), C)
        return pltpu.make_async_remote_copy(
            src_ref=part.at[mb, rows],
            dst_ref=buf.at[mb, NX - k],
            send_sem=rs_send.at[kind, mb, k],
            recv_sem=rs_recv.at[kind, mb, NX - k],
            device_id={"tp": h * NX + peer_x(k)},
            device_id_type=MESH,
        )

    def rs_wait(part, buf, kind, mb, k):
        rows = pl.ds(pl.multiple_of(peer_x(k) * C, C), C)
        pltpu.make_async_remote_copy(
            src_ref=part.at[mb, rows],
            dst_ref=buf.at[mb, k],
            send_sem=rs_send.at[kind, mb, k],
            recv_sem=rs_recv.at[kind, mb, k],
            device_id={"tp": h * NX + peer_x(k)},
            device_id_type=MESH,
        ).wait_recv()

    def z_copy(src, buf, kind, mb, hh):
        to = s + 1 if kind == 0 else s - 1
        return pltpu.make_async_remote_copy(
            src_ref=src.at[mb],
            dst_ref=buf.at[mb, h],
            send_sem=z_send.at[kind, mb, hh],
            recv_sem=z_recv.at[kind, mb, h],
            device_id={"section": to % SECTIONS, "tp": hh * NX + x},
            device_id_type=MESH,
        )

    def z_wait(src, buf, kind, mb, hh):
        pltpu.make_async_remote_copy(
            src_ref=src.at[mb],
            dst_ref=buf.at[mb, hh],
            send_sem=z_send.at[kind, mb, hh],
            recv_sem=z_recv.at[kind, mb, hh],
            device_id={"tp": (1 - h) * NX + x},
            device_id_type=MESH,
        ).wait_recv()

    def o_copy(ost, orecv, kind, mb, k):
        who = (t + k) % TP
        return pltpu.make_async_remote_copy(
            src_ref=ost.at[mb, who],
            dst_ref=orecv.at[h, mb, x],
            send_sem=o_send.at[kind, mb, k],
            recv_sem=o_recv.at[kind, mb, TP - k],
            device_id={"tp": who},
            device_id_type=MESH,
        )

    def o_wait(ost, orecv, kind, mb, k):
        who = (t + k) % TP
        pltpu.make_async_remote_copy(
            src_ref=ost.at[mb, who],
            dst_ref=orecv.at[who // NX, mb, who % NX],
            send_sem=o_send.at[kind, mb, k],
            recv_sem=o_recv.at[kind, mb, k],
            device_id={"tp": who},
            device_id_type=MESH,
        ).wait_recv()

    far_first = (2, 1, 3)

    def step_first(piece):
        @pl.when(piece == 0)
        def _():
            for load in loads[:3]:
                load.wait()

        @pl.when(s == 0)
        def _():
            gather_blocks(acts, piece)
            for b in range(MB // 2):
                mb = piece * (MB // 2) + b
                xf, rms = rms_parts(full[pl.ds(pl.multiple_of(mb * R, R), R), :])
                nb[mb] = (xf / rms).astype(BF16)
                xrow[mb] = full[pl.ds(pl.multiple_of(mb * R + x * C, C), C), :]

        @pl.when(s == SECTIONS - 1)
        def _():
            gather_blocks(cot, piece)
            for b in range(MB // 2):
                mb = piece * (MB // 2) + b
                dyb[mb] = full[pl.ds(pl.multiple_of(mb * R, R), R), :]
                dyrow[mb] = full[pl.ds(pl.multiple_of(mb * R + x * C, C), C), :]

    def head_fwd(mb):
        @pl.when(s > 0)
        def _():
            z_wait(zsend_f, zrecv_f, 0, mb, 0)
            z_wait(zsend_f, zrecv_f, 0, mb, 1)
            rows = (zrecv_f[mb, 0].astype(F32) + zrecv_f[mb, 1].astype(F32)).astype(BF16)
            xrow[mb] = rows
            xf, rms = rms_parts(rows)
            nb[mb, own] = (xf / rms).astype(BF16)
            for k in far_first:
                ag_copy(nb, 0, mb, k).start()

    def main_fwd(mb):
        @pl.when(s > 0)
        def _():
            for k in (1, 3, 2):
                ag_wait(nb, 0, mb, k)

        normed = nb[mb]
        gate = dot_nt(normed, wg[...]) * INV_D
        upper = dot_nt(normed, wu[...]) * INV_D
        sig = jax.nn.sigmoid(gate)
        active = gate * sig
        hidden = (active * upper).astype(BF16)
        part_f[mb] = (dot_nn(hidden, wd[...]) * INV_FF).astype(BF16)
        for k in far_first:
            rs_copy(part_f, rs_f, 0, mb, k).start()
        hidden_s[mb] = hidden
        act_s[mb] = active
        slope_s[mb] = upper * sig * (1.0 + gate * (1.0 - sig))

    def half_sum(part, buf, kind, mb):
        for k in (1, 3, 2):
            rs_wait(part, buf, kind, mb, k)
        total = part[mb, own].astype(F32)
        for k in range(1, NX):
            total = total + buf[mb, k].astype(F32)
        return total

    def tail_fwd(mb):
        half = half_sum(part_f, rs_f, 0, mb)
        zsend_f[mb] = (half + 0.5 * xrow[mb].astype(F32)).astype(BF16)

        @pl.when(s < SECTIONS - 1)
        def _():
            z_copy(zsend_f, zrecv_f, 0, mb, 0).start()
            z_copy(zsend_f, zrecv_f, 0, mb, 1).start()

    def head_bwd(mb):
        @pl.when(s < SECTIONS - 1)
        def _():
            z_wait(zsend_b, zrecv_b, 1, mb, 0)
            z_wait(zsend_b, zrecv_b, 1, mb, 1)
            rows = (zrecv_b[mb, 0].astype(F32) + zrecv_b[mb, 1].astype(F32)).astype(BF16)
            dyrow[mb] = rows
            dyb[mb, own] = rows
            for k in far_first:
                ag_copy(dyb, 1, mb, k).start()

    def main_bwd(mb):
        @pl.when(s < SECTIONS - 1)
        def _():
            for k in (1, 3, 2):
                ag_wait(dyb, 1, mb, k)

        dh = dot_nt(dyb[mb], wd[...]) * INV_FF
        dgate = (dh * slope_s[mb]).astype(BF16)
        dup = (dh * act_s[mb]).astype(BF16)
        part_b[mb] = ((dot_nn(dgate, wg[...]) + dot_nn(dup, wu[...])) * INV_D).astype(BF16)
        for k in far_first:
            rs_copy(part_b, rs_b, 1, mb, k).start()
        dgate_s[mb] = dgate
        dup_s[mb] = dup

    def tail_bwd(mb):
        xf, rms = rms_parts(xrow[mb])
        normed = xf / rms
        half = half_sum(part_b, rs_b, 1, mb)
        stat = jnp.sum(half * normed, axis=1, keepdims=True) / D
        grad = 0.5 * dyrow[mb].astype(F32) + (half - normed * stat) / rms
        zsend_b[mb] = grad.astype(BF16)

        @pl.when(s > 0)
        def _():
            z_copy(zsend_b, zrecv_b, 1, mb, 0).start()
            z_copy(zsend_b, zrecv_b, 1, mb, 1).start()

    def spread_columns(zsend, ost, orecv, kind, mb):
        wide = dot_nn(zsend[mb], spread[...]).astype(BF16)
        for q in range(TP):
            ost[mb, q] = wide[:, q * 128 : (q + 1) * 128]
        orecv[h, mb, x] = ost[mb, t]
        for k in order:
            o_copy(ost, orecv, kind, mb, k).start()

    def out_fwd(mb):
        @pl.when(mb == 0)
        def _():
            feature = lax.broadcasted_iota(jnp.int32, (D, TP * 128), 0)
            place = lax.broadcasted_iota(jnp.int32, (D, TP * 128), 1)
            lane = place % 128
            hit = (feature == (place // 128) * BLOCK + lane) & (lane < BLOCK)
            spread[...] = jnp.where(hit, 1.0, 0.0).astype(BF16)

        spread_columns(zsend_f, ost_f, orecv_f, 0, mb)

    def out_bwd(mb):
        spread_columns(zsend_b, ost_b, orecv_b, 1, mb)

    def update(number, units, rows, scale, weight, first, second, new):
        loads[3 + 2 * number].wait()
        loads[4 + 2 * number].wait()
        hid = weight.shape[0]
        grad[...] = dot_tn(units[...].reshape(ROWS, hid), rows[...].reshape(ROWS, D)) * scale

        def piece(index, carry):
            part = pl.ds(pl.multiple_of(index * 32, 32), 32)
            g = grad[part, :]
            m_new = BETA_ONE * first[part, :].astype(F32) + (1.0 - BETA_ONE) * g
            v_new = BETA_TWO * second[part, :].astype(F32) + (1.0 - BETA_TWO) * g * g
            step = LEARN * m_new / (jnp.sqrt(v_new) + ADAM_EPS)
            new[part, :] = (weight[part, :].astype(F32) - step).astype(BF16)
            return carry

        lax.fori_loop(0, hid // 32, piece, 0)
        stores[number].start()

    def update_down(mb):
        update(0, hidden_s, dyb, INV_FF, wd, md, vd, nd)

    def update_gate(mb):
        update(1, dgate_s, nb, INV_D, wg, mg, vg, ng)

    def update_up(mb):
        update(2, dup_s, nb, INV_D, wu, mu, vu, nu)

    def finish(mb):
        for kind, ost, orecv, out in ((0, ost_f, orecv_f, out_y), (1, ost_b, orecv_b, out_dx)):
            for b in range(MB):
                for k in range(1, TP):
                    o_wait(ost, orecv, kind, b, k)
            halves = orecv[...].reshape(2, ROWS, 128).astype(F32)
            out[...] = (halves[0] + halves[1]).T[:BLOCK].astype(BF16)

    steps = (
        step_first,
        head_fwd,
        main_fwd,
        tail_fwd,
        head_bwd,
        main_bwd,
        tail_bwd,
        out_fwd,
        out_bwd,
        update_down,
        update_gate,
        update_up,
        finish,
    )

    def run(index, carry):
        code = jnp.int32(0)
        mb = jnp.int32(0)
        for place, (first, middle, last) in enumerate(zip(FIRST, MIDDLE, LAST)):
            here = index == place
            for field in range(2):
                value = jnp.where(s == SECTIONS - 1, last[field], middle[field])
                value = jnp.where(s == 0, first[field], value)
                if field == 0:
                    code = jnp.where(here, value, code)
                else:
                    mb = jnp.where(here, value, mb)
        for number, step in enumerate(steps):

            @pl.when(code == number)
            def _(step=step):
                step(mb)

        return carry

    lax.fori_loop(0, len(MIDDLE), run, 0)

    for store in stores:
        store.wait()

    @pl.when(s == 0)
    def _():
        for piece in range(2):
            for k in order:
                in_copy(acts, piece, k).wait_send()

    @pl.when(s == SECTIONS - 1)
    def _():
        for piece in range(2):
            for k in order:
                in_copy(cot, piece, k).wait_send()

    def drain(mb, carry):
        for k in far_first:
            rs_copy(part_f, rs_f, 0, mb, k).wait_send()
            rs_copy(part_b, rs_b, 1, mb, k).wait_send()
        for k in range(1, TP):
            o_copy(ost_f, orecv_f, 0, mb, k).wait_send()
            o_copy(ost_b, orecv_b, 1, mb, k).wait_send()

        @pl.when(s > 0)
        def _():
            for k in far_first:
                ag_copy(nb, 0, mb, k).wait_send()
            for hh in range(2):
                z_copy(zsend_b, zrecv_b, 1, mb, hh).wait_send()

        @pl.when(s < SECTIONS - 1)
        def _():
            for k in far_first:
                ag_copy(dyb, 1, mb, k).wait_send()
            for hh in range(2):
                z_copy(zsend_f, zrecv_f, 0, mb, hh).wait_send()

        return carry

    lax.fori_loop(0, MB, drain, 0)


def chain(acts, cot, weights, firsts, seconds):
    hid = weights[0].shape[0]
    vm = pl.BlockSpec(memory_space=pltpu.VMEM)
    hbm = pl.BlockSpec(memory_space=pl.ANY)
    shape = jax.ShapeDtypeStruct
    dma = pltpu.SemaphoreType.DMA
    return pl.pallas_call(
        chain_kernel,
        out_shape=(shape((BLOCK, ROWS), BF16),) * 2 + (shape((hid, D), BF16),) * 3,
        in_specs=[vm] * 2 + [hbm] * 9,
        out_specs=[vm] * 2 + [hbm] * 3,
        scratch_shapes=[pltpu.VMEM((hid, D), BF16)] * 12
        + [
            pltpu.VMEM((hid, D), F32),
            pltpu.VMEM((D, ROWS), BF16),
            pltpu.VMEM((ROWS, D), BF16),
            pltpu.VMEM((MB, R, hid), BF16),
            pltpu.VMEM((MB, R, hid), BF16),
            pltpu.VMEM((MB, R, hid), BF16),
            pltpu.VMEM((MB, R, hid), F32),
            pltpu.VMEM((MB, R, hid), F32),
            pltpu.VMEM((D, TP * 128), BF16),
            pltpu.VMEM((MB, R, D), BF16),
            pltpu.VMEM((MB, R, D), BF16),
            pltpu.VMEM((MB, C, D), BF16),
            pltpu.VMEM((MB, C, D), BF16),
            pltpu.VMEM((MB, R, D), BF16),
            pltpu.VMEM((MB, R, D), BF16),
            pltpu.VMEM((MB, NX, C, D), BF16),
            pltpu.VMEM((MB, NX, C, D), BF16),
            pltpu.VMEM((MB, C, D), BF16),
            pltpu.VMEM((MB, C, D), BF16),
            pltpu.VMEM((MB, 2, C, D), BF16),
            pltpu.VMEM((MB, 2, C, D), BF16),
            pltpu.VMEM((MB, TP, C, 128), BF16),
            pltpu.VMEM((MB, TP, C, 128), BF16),
            pltpu.VMEM((2, MB, NX, C, 128), BF16),
            pltpu.VMEM((2, MB, NX, C, 128), BF16),
            dma((9,)),
            dma((3,)),
            dma((2, TP)),
            dma((2, TP)),
            dma((2, MB, NX)),
            dma((2, MB, NX)),
            dma((2, MB, NX)),
            dma((2, MB, NX)),
            dma((2, MB, 2)),
            dma((2, MB, 2)),
            dma((2, MB, TP)),
            dma((2, MB, TP)),
        ],
        compiler_params=pltpu.CompilerParams(
            collective_id=0, has_side_effects=True, vmem_limit_bytes=56 * 1024 * 1024
        ),
        name="chain",
    )(acts, cot, *weights, *firsts, *seconds)


def mean(own, other):
    return ((own.astype(F32) + other.astype(F32)) * 0.5).astype(BF16)


def gossip(*updated, distance):
    peers = lax.axis_size("rep")
    pairs = [(i, (i + distance) % peers) for i in range(peers)]
    means = tuple(mean(own, lax.ppermute(own, "rep", pairs)) for own in updated)
    return lax.optimization_barrier(means)


def on_device(
    acts, cotangent, w_gate, w_up, w_down, m_gate, m_up, m_down, v_gate, v_up, v_down, steps
):
    def by_units(gate, up, down):
        return gate[0, 0].T, up[0, 0].T, down[0, 0]

    y, dx, *updated = chain(
        acts[0].T,
        cotangent[0].T,
        by_units(w_gate, w_up, w_down),
        by_units(m_gate, m_up, m_down),
        by_units(v_gate, v_up, v_down),
    )
    levels = lax.axis_size("rep").bit_length() - 1
    branches = [functools.partial(gossip, distance=2**level) for level in range(levels)]
    new_gate, new_up, new_down = lax.switch(steps[0] % levels, branches, *updated)
    return (
        y.T[None, None],
        dx.T[None, None],
        new_gate.T[None, None],
        new_up.T[None, None],
        new_down[None, None],
    )


def solution(mesh):
    return jax.shard_map(
        on_device,
        mesh=mesh,
        in_specs=(
            P("rep", None, "tp"),
            P("rep", None, "tp"),
            P("section", "rep", None, "tp"),
            P("section", "rep", None, "tp"),
            P("section", "rep", "tp", None),
            P("section", "rep", None, "tp"),
            P("section", "rep", None, "tp"),
            P("section", "rep", "tp", None),
            P("section", "rep", None, "tp"),
            P("section", "rep", None, "tp"),
            P("section", "rep", "tp", None),
            P("section"),
        ),
        out_specs=(
            P("section", "rep", None, "tp"),
            P("section", "rep", None, "tp"),
            P("section", "rep", None, "tp"),
            P("section", "rep", None, "tp"),
            P("section", "rep", "tp", None),
        ),
        check_vma=False,
    )
```

```python
import functools
import math

import jax
import jax.numpy as jnp
from jax import lax
from jax.experimental import pallas as pl
from jax.experimental.pallas import tpu as pltpu
from jax.sharding import PartitionSpec as P

D = 896
FF = 4864
ROWS = 256
SECTIONS = 4
TP = 8
NX = 4
BLOCK = D // TP
MB = 4
R = ROWS // MB
HALF = ROWS // 2
RELAYED = 384
C = R // NX

NORM_EPS = 1e-06
ADAM_EPS = 1e-08
LEARN = 0.3
BETA_ONE = 0.9
BETA_TWO = 0.95
INV_D = 1.0 / math.sqrt(D)
INV_FF = 1.0 / math.sqrt(FF)
MESH = pl.DeviceIdType.MESH
BF16 = jnp.bfloat16
F32 = jnp.float32

CODES = {name: number for number, name in enumerate("IHMThmtOoDGUE-")}


PER_WORD = 5


def plan(text):
    return [CODES[name] * MB + int(mb) for name, mb in zip(text[::2], text[1::2])]


def packed(steps):
    words = [steps[at : at + PER_WORD] for at in range(0, len(steps), PER_WORD)]
    return [sum(step << (6 * place) for place, step in enumerate(word)) for word in words]


START = "I0H0H1M0I1H2M1H3T0M2T1M3T2T3"
RETURN = "O0O1O2O3h0h1m0h2m1h3t0m2t1m3t2"
FIRST = plan(START + "O0O1O2O3h0h1m0h2m1h3m2m3D0G0U0E0")
MIDDLE = plan(START + RETURN + "t3o0o1o2o3D0G0U0E0")
FIRST = FIRST + plan("-0") * (len(MIDDLE) - len(FIRST))
TURN = plan("I0I1H0H1M0m0H2M1m1t0H3M2m2t1M3m3t2t3")
LAST = TURN + plan("D0G0U0T0T1T2T3O0O1O2O3o0o1o2o3E0")
LAST = LAST + plan("-0") * (len(MIDDLE) - len(LAST))


def rms_parts(rows):
    xf = rows.astype(F32)
    rms = jnp.sqrt(jnp.mean(xf * xf, axis=1, keepdims=True) + NORM_EPS)
    return xf, rms


def dot_nn(left, right):
    return lax.dot_general(left, right, (((1,), (0,)), ((), ())), preferred_element_type=F32)


def dot_tn(left, right):
    return lax.dot_general(left, right, (((0,), (0,)), ((), ())), preferred_element_type=F32)


def dot_nt(left, right):
    return lax.dot_general(left, right, (((1,), (1,)), ((), ())), preferred_element_type=F32)


def chain_kernel(
    acts,
    cot,
    wg_hbm,
    wu_hbm,
    wd_hbm,
    mg_hbm,
    mu_hbm,
    md_hbm,
    vg_hbm,
    vu_hbm,
    vd_hbm,
    out_y,
    out_dx,
    out_gate,
    out_up,
    out_part,
    out_rest,
    wg,
    wu,
    wd,
    mg,
    mu,
    md,
    vg,
    vu,
    vd,
    ng,
    nu,
    nd,
    grad,
    xin,
    full,
    hidden_s,
    dgate_s,
    dup_s,
    act_s,
    slope_s,
    spread,
    nb,
    dyb,
    xrow,
    dyrow,
    part_f,
    part_b,
    rs_f,
    rs_b,
    zsend_f,
    zsend_b,
    zrecv_f,
    zrecv_b,
    ost_f,
    ost_b,
    orecv_f,
    orecv_b,
    ost_x,
    orecv_x,
    load_sem,
    store_sem,
    in_send,
    in_recv,
    ag_send,
    ag_recv,
    rs_send,
    rs_recv,
    z_send,
    z_recv,
    o_send,
    o_recv,
):
    s = lax.axis_index("section")
    t = lax.axis_index("tp")
    h = t // NX
    x = t % NX
    own = pl.ds(pl.multiple_of(x * C, C), C)

    def at_tp(where):
        return {"tp": where}

    def peer_x(k):
        return (x + k) % NX

    loads = [
        pltpu.make_async_copy(src, dst, load_sem.at[number])
        for number, (src, dst) in enumerate(
            (
                (wg_hbm, wg),
                (wu_hbm, wu),
                (wd_hbm, wd),
                (md_hbm, md),
                (vd_hbm, vd),
                (mg_hbm, mg),
                (vg_hbm, vg),
                (mu_hbm, mu),
                (vu_hbm, vu),
            )
        )
    ]
    stores = [
        pltpu.make_async_copy(src, dst, store_sem.at[number])
        for number, (src, dst) in enumerate(
            (
                (nd.at[:RELAYED], out_part),
                (nd.at[RELAYED:], out_rest),
                (ng, out_gate),
                (nu, out_up),
            )
        )
    ]
    for load in loads[:3]:
        load.start()

    barrier = pltpu.get_barrier_semaphore()
    for k in range(1, TP):
        pl.semaphore_signal(barrier, inc=1, device_id={"tp": (t + k) % TP}, device_id_type=MESH)
    for step in (1, SECTIONS - 1):
        for hh in range(2):
            pl.semaphore_signal(
                barrier,
                inc=1,
                device_id={"section": (s + step) % SECTIONS, "tp": hh * NX + x},
                device_id_type=MESH,
            )
    pl.semaphore_wait(barrier, TP - 1 + 4)

    def block_of(who):
        return pl.ds(pl.multiple_of(who * BLOCK, BLOCK), BLOCK)

    def half_of(piece):
        return pl.ds(pl.multiple_of(piece * HALF, HALF), HALF)

    def in_copy(src, piece, k):
        return pltpu.make_async_remote_copy(
            src_ref=src.at[:, half_of(piece)],
            dst_ref=xin.at[block_of(t), half_of(piece)],
            send_sem=in_send.at[piece, k],
            recv_sem=in_recv.at[piece, t],
            device_id={"tp": (t + k) % TP},
            device_id_type=MESH,
        )

    def in_wait(piece, k):
        who = (t + k) % TP
        pltpu.make_async_remote_copy(
            src_ref=xin.at[block_of(who), half_of(piece)],
            dst_ref=xin.at[block_of(who), half_of(piece)],
            send_sem=in_send.at[piece, k],
            recv_sem=in_recv.at[piece, who],
            device_id={"tp": who},
            device_id_type=MESH,
        ).wait_recv()

    order = (4, 5, 3, 6, 2, 7, 1)

    @pl.when(s == 0)
    def _():
        for piece in range(2):
            for k in order:
                in_copy(acts, piece, k).start()

    @pl.when(s == SECTIONS - 1)
    def _():
        for piece in range(2):
            for k in order:
                in_copy(cot, piece, k).start()

    for load in loads[3:]:
        load.start()

    def gather_blocks(src, piece):
        xin[block_of(t), half_of(piece)] = src[:, half_of(piece)]
        for k in range(1, TP):
            in_wait(piece, k)
        full[half_of(piece), :] = xin[:, half_of(piece)].astype(F32).T.astype(BF16)

    def ag_copy(buf, kind, mb, k):
        return pltpu.make_async_remote_copy(
            src_ref=buf.at[mb, own],
            dst_ref=buf.at[mb, own],
            send_sem=ag_send.at[kind, mb, k],
            recv_sem=ag_recv.at[kind, mb, NX - k],
            device_id={"tp": h * NX + peer_x(k)},
            device_id_type=MESH,
        )

    def ag_wait(buf, kind, mb, k):
        rows = pl.ds(pl.multiple_of(peer_x(k) * C, C), C)
        pltpu.make_async_remote_copy(
            src_ref=buf.at[mb, rows],
            dst_ref=buf.at[mb, rows],
            send_sem=ag_send.at[kind, mb, k],
            recv_sem=ag_recv.at[kind, mb, k],
            device_id={"tp": h * NX + peer_x(k)},
            device_id_type=MESH,
        ).wait_recv()

    def rs_copy(part, buf, kind, mb, k):
        rows = pl.ds(pl.multiple_of(peer_x(k) * C, C), C)
        return pltpu.make_async_remote_copy(
            src_ref=part.at[mb, rows],
            dst_ref=buf.at[mb, NX - k],
            send_sem=rs_send.at[kind, mb, k],
            recv_sem=rs_recv.at[kind, mb, NX - k],
            device_id={"tp": h * NX + peer_x(k)},
            device_id_type=MESH,
        )

    def rs_wait(part, buf, kind, mb, k):
        rows = pl.ds(pl.multiple_of(peer_x(k) * C, C), C)
        pltpu.make_async_remote_copy(
            src_ref=part.at[mb, rows],
            dst_ref=buf.at[mb, k],
            send_sem=rs_send.at[kind, mb, k],
            recv_sem=rs_recv.at[kind, mb, k],
            device_id={"tp": h * NX + peer_x(k)},
            device_id_type=MESH,
        ).wait_recv()

    def z_copy(src, buf, kind, mb, hh):
        to = s + 1 if kind == 0 else s - 1
        return pltpu.make_async_remote_copy(
            src_ref=src.at[mb],
            dst_ref=buf.at[mb, h],
            send_sem=z_send.at[kind, mb, hh],
            recv_sem=z_recv.at[kind, mb, h],
            device_id={"section": to % SECTIONS, "tp": hh * NX + x},
            device_id_type=MESH,
        )

    def z_wait(src, buf, kind, mb, hh):
        pltpu.make_async_remote_copy(
            src_ref=src.at[mb],
            dst_ref=buf.at[mb, hh],
            send_sem=z_send.at[kind, mb, hh],
            recv_sem=z_recv.at[kind, mb, hh],
            device_id={"tp": (1 - h) * NX + x},
            device_id_type=MESH,
        ).wait_recv()

    def o_copy(ost, orecv, kind, mb, k):
        who = (t + k) % TP
        return pltpu.make_async_remote_copy(
            src_ref=ost.at[mb, who],
            dst_ref=orecv.at[h, mb, x],
            send_sem=o_send.at[kind, mb, k],
            recv_sem=o_recv.at[kind, mb, TP - k],
            device_id={"tp": who},
            device_id_type=MESH,
        )

    def x_copy(mb, k):
        who = (t + k) % TP
        return pltpu.make_async_remote_copy(
            src_ref=ost_x.at[mb, who],
            dst_ref=orecv_x.at[t, mb],
            send_sem=o_send.at[1, mb, k],
            recv_sem=o_recv.at[1, mb, TP - k],
            device_id={"tp": who},
            device_id_type=MESH,
        )

    def x_wait(mb, k):
        who = (t + k) % TP
        pltpu.make_async_remote_copy(
            src_ref=ost_x.at[mb, who],
            dst_ref=orecv_x.at[who, mb],
            send_sem=o_send.at[1, mb, k],
            recv_sem=o_recv.at[1, mb, k],
            device_id={"tp": who},
            device_id_type=MESH,
        ).wait_recv()

    def o_wait(ost, orecv, kind, mb, k):
        who = (t + k) % TP
        pltpu.make_async_remote_copy(
            src_ref=ost.at[mb, who],
            dst_ref=orecv.at[who // NX, mb, who % NX],
            send_sem=o_send.at[kind, mb, k],
            recv_sem=o_recv.at[kind, mb, k],
            device_id={"tp": who},
            device_id_type=MESH,
        ).wait_recv()

    far_first = (2, 1, 3)

    def step_first(piece):
        @pl.when(piece == 0)
        def _():
            for load in loads[:3]:
                load.wait()

        @pl.when(s == 0)
        def _():
            gather_blocks(acts, piece)
            for b in range(MB // 2):
                mb = piece * (MB // 2) + b
                xf, rms = rms_parts(full[pl.ds(pl.multiple_of(mb * R, R), R), :])
                nb[mb] = (xf / rms).astype(BF16)
                xrow[mb] = full[pl.ds(pl.multiple_of(mb * R + x * C, C), C), :]

        @pl.when(s == SECTIONS - 1)
        def _():
            gather_blocks(cot, piece)
            for b in range(MB // 2):
                mb = piece * (MB // 2) + b
                dyb[mb] = full[pl.ds(pl.multiple_of(mb * R, R), R), :]
                dyrow[mb] = full[pl.ds(pl.multiple_of(mb * R + x * C, C), C), :]

    def head_fwd(mb):
        @pl.when(s > 0)
        def _():
            z_wait(zsend_f, zrecv_f, 0, mb, 0)
            z_wait(zsend_f, zrecv_f, 0, mb, 1)
            rows = (zrecv_f[mb, 0].astype(F32) + zrecv_f[mb, 1].astype(F32)).astype(BF16)
            xrow[mb] = rows
            xf, rms = rms_parts(rows)
            nb[mb, own] = (xf / rms).astype(BF16)
            for k in far_first:
                ag_copy(nb, 0, mb, k).start()

    def main_fwd(mb):
        @pl.when(s > 0)
        def _():
            for k in (1, 3, 2):
                ag_wait(nb, 0, mb, k)

        normed = nb[mb]
        gate = dot_nt(normed, wg[...]) * INV_D
        upper = dot_nt(normed, wu[...]) * INV_D
        sig = jax.nn.sigmoid(gate)
        active = gate * sig
        hidden = (active * upper).astype(BF16)
        part_f[mb] = (dot_nn(hidden, wd[...]) * INV_FF).astype(BF16)
        for k in far_first:
            rs_copy(part_f, rs_f, 0, mb, k).start()
        hidden_s[mb] = hidden
        act_s[mb] = active
        slope_s[mb] = upper * sig * (1.0 + gate * (1.0 - sig))

    def half_sum(part, buf, kind, mb):
        for k in (1, 3, 2):
            rs_wait(part, buf, kind, mb, k)
        total = part[mb, own].astype(F32)
        for k in range(1, NX):
            total = total + buf[mb, k].astype(F32)
        return total

    def tail_fwd(mb):
        half = half_sum(part_f, rs_f, 0, mb)
        zsend_f[mb] = (half + 0.5 * xrow[mb].astype(F32)).astype(BF16)

        @pl.when(s < SECTIONS - 1)
        def _():
            z_copy(zsend_f, zrecv_f, 0, mb, 0).start()
            z_copy(zsend_f, zrecv_f, 0, mb, 1).start()

    def head_bwd(mb):
        @pl.when(s < SECTIONS - 1)
        def _():
            z_wait(zsend_b, zrecv_b, 1, mb, 0)
            z_wait(zsend_b, zrecv_b, 1, mb, 1)
            rows = (zrecv_b[mb, 0].astype(F32) + zrecv_b[mb, 1].astype(F32)).astype(BF16)
            dyrow[mb] = rows
            dyb[mb, own] = rows
            for k in far_first:
                ag_copy(dyb, 1, mb, k).start()

    def main_bwd(mb):
        @pl.when(s < SECTIONS - 1)
        def _():
            for k in (1, 3, 2):
                ag_wait(dyb, 1, mb, k)

        dh = dot_nt(dyb[mb], wd[...]) * INV_FF
        dgate = (dh * slope_s[mb]).astype(BF16)
        dup = (dh * act_s[mb]).astype(BF16)
        part = (dot_nn(dgate, wg[...]) + dot_nn(dup, wu[...])) * INV_D

        @pl.when(s > 0)
        def _():
            part_b[mb] = part.astype(BF16)
            for k in far_first:
                rs_copy(part_b, rs_b, 1, mb, k).start()

        @pl.when(s == 0)
        def _():
            xf, rms = rms_parts(full[pl.ds(pl.multiple_of(mb * R, R), R), :])
            normed = xf / rms
            stat = jnp.sum(part * normed, axis=1, keepdims=True) / D
            share = dyb[mb].astype(F32) * (1.0 / TP) + (part - normed * stat) / rms
            wide = dot_nn(share.astype(BF16), spread[...]).astype(BF16)
            for q in range(TP):
                ost_x[mb, q] = wide[:, q * 128 : (q + 1) * 128]
            orecv_x[t, mb] = ost_x[mb, t]
            for k in order:
                x_copy(mb, k).start()

        dgate_s[mb] = dgate
        dup_s[mb] = dup

    def tail_bwd(mb):
        xf, rms = rms_parts(xrow[mb])
        normed = xf / rms
        half = half_sum(part_b, rs_b, 1, mb)
        stat = jnp.sum(half * normed, axis=1, keepdims=True) / D
        grad = 0.5 * dyrow[mb].astype(F32) + (half - normed * stat) / rms
        zsend_b[mb] = grad.astype(BF16)

        z_copy(zsend_b, zrecv_b, 1, mb, 0).start()
        z_copy(zsend_b, zrecv_b, 1, mb, 1).start()

    def spread_columns(zsend, ost, orecv, kind, mb):
        wide = dot_nn(zsend[mb], spread[...]).astype(BF16)
        for q in range(TP):
            ost[mb, q] = wide[:, q * 128 : (q + 1) * 128]
        orecv[h, mb, x] = ost[mb, t]
        for k in order:
            o_copy(ost, orecv, kind, mb, k).start()

    def out_fwd(mb):
        @pl.when(mb == 0)
        def _():
            feature = lax.broadcasted_iota(jnp.int32, (D, TP * 128), 0)
            place = lax.broadcasted_iota(jnp.int32, (D, TP * 128), 1)
            lane = place % 128
            hit = (feature == (place // 128) * BLOCK + lane) & (lane < BLOCK)
            spread[...] = jnp.where(hit, 1.0, 0.0).astype(BF16)

        spread_columns(zsend_f, ost_f, orecv_f, 0, mb)

    def out_bwd(mb):
        spread_columns(zsend_b, ost_b, orecv_b, 1, mb)

    def update(number, units, rows, scale, weight, first, second, new):
        loads[3 + 2 * number].wait()
        loads[4 + 2 * number].wait()
        hid = weight.shape[0]
        grad[...] = dot_tn(units[...].reshape(ROWS, hid), rows[...].reshape(ROWS, D)) * scale

        def piece(index, carry):
            part = pl.ds(pl.multiple_of(index * 32, 32), 32)
            g = grad[part, :]
            m_new = BETA_ONE * first[part, :].astype(F32) + (1.0 - BETA_ONE) * g
            v_new = BETA_TWO * second[part, :].astype(F32) + (1.0 - BETA_TWO) * g * g
            step = LEARN * m_new / (jnp.sqrt(v_new) + ADAM_EPS)
            new[part, :] = (weight[part, :].astype(F32) - step).astype(BF16)
            return carry

        lax.fori_loop(0, hid // 32, piece, 0)
        for store in stores[:2] if number == 0 else stores[number + 1 : number + 2]:
            store.start()

    def update_down(mb):
        update(0, hidden_s, dyb, INV_FF, wd, md, vd, nd)

    def update_gate(mb):
        update(1, dgate_s, nb, INV_D, wg, mg, vg, ng)

    def update_up(mb):
        update(2, dup_s, nb, INV_D, wu, mu, vu, nu)

    def finish(mb):
        def columns(kind, ost, orecv, out):
            for b in range(MB):
                for k in range(1, TP):
                    o_wait(ost, orecv, kind, b, k)
            halves = orecv[...].reshape(2, ROWS, 128).astype(F32)
            out[...] = (halves[0] + halves[1]).T[:BLOCK].astype(BF16)

        columns(0, ost_f, orecv_f, out_y)

        @pl.when(s > 0)
        def _():
            columns(1, ost_b, orecv_b, out_dx)

        @pl.when(s == 0)
        def _():
            for b in range(MB):
                for k in range(1, TP):
                    x_wait(b, k)
            total = orecv_x[0].reshape(ROWS, 128).astype(F32)
            for q in range(1, TP):
                total = total + orecv_x[q].reshape(ROWS, 128).astype(F32)
            out_dx[...] = total.T[:BLOCK].astype(BF16)

    steps = (
        step_first,
        head_fwd,
        main_fwd,
        tail_fwd,
        head_bwd,
        main_bwd,
        tail_bwd,
        out_fwd,
        out_bwd,
        update_down,
        update_gate,
        update_up,
        finish,
        lambda mb: None,
    )

    words = [
        jnp.where(s == 0, first, jnp.where(s == SECTIONS - 1, last, middle))
        for first, middle, last in zip(packed(FIRST), packed(MIDDLE), packed(LAST))
    ]

    def run(index, carry):
        word = words[0]
        for place in range(1, len(words)):
            word = jnp.where(index // PER_WORD == place, words[place], word)
        step = (word >> (6 * (index % PER_WORD))) & 63
        mb = step % MB
        code = step // MB

        def dispatch(low, high):
            if high - low == 1:
                steps[low](mb)
                return
            middle = (low + high) // 2

            @pl.when(code < middle)
            def _():
                dispatch(low, middle)

            @pl.when(code >= middle)
            def _():
                dispatch(middle, high)

        dispatch(0, len(steps))
        return carry

    lax.fori_loop(0, len(MIDDLE), run, 0)

    for store in stores:
        store.wait()

    @pl.when(s == 0)
    def _():
        for piece in range(2):
            for k in order:
                in_copy(acts, piece, k).wait_send()

    @pl.when(s == SECTIONS - 1)
    def _():
        for piece in range(2):
            for k in order:
                in_copy(cot, piece, k).wait_send()

    def drain(mb, carry):
        for k in far_first:
            rs_copy(part_f, rs_f, 0, mb, k).wait_send()
        for k in range(1, TP):
            o_copy(ost_f, orecv_f, 0, mb, k).wait_send()

        @pl.when(s == 0)
        def _():
            for k in range(1, TP):
                x_copy(mb, k).wait_send()

        @pl.when(s > 0)
        def _():
            for k in far_first:
                ag_copy(nb, 0, mb, k).wait_send()
                rs_copy(part_b, rs_b, 1, mb, k).wait_send()
            for k in range(1, TP):
                o_copy(ost_b, orecv_b, 1, mb, k).wait_send()
            for hh in range(2):
                z_copy(zsend_b, zrecv_b, 1, mb, hh).wait_send()

        @pl.when(s < SECTIONS - 1)
        def _():
            for k in far_first:
                ag_copy(dyb, 1, mb, k).wait_send()
            for hh in range(2):
                z_copy(zsend_f, zrecv_f, 0, mb, hh).wait_send()

        return carry

    lax.fori_loop(0, MB, drain, 0)


def chain(acts, cot, weights, firsts, seconds):
    hid = weights[0].shape[0]
    vm = pl.BlockSpec(memory_space=pltpu.VMEM)
    hbm = pl.BlockSpec(memory_space=pl.ANY)
    shape = jax.ShapeDtypeStruct
    dma = pltpu.SemaphoreType.DMA
    return pl.pallas_call(
        chain_kernel,
        out_shape=(shape((BLOCK, ROWS), BF16),) * 2
        + (shape((hid, D), BF16),) * 2
        + (shape((RELAYED, D), BF16), shape((hid - RELAYED, D), BF16)),
        in_specs=[vm] * 2 + [hbm] * 9,
        out_specs=[vm] * 2 + [hbm] * 4,
        scratch_shapes=[pltpu.VMEM((hid, D), BF16)] * 12
        + [
            pltpu.VMEM((hid, D), F32),
            pltpu.VMEM((D, ROWS), BF16),
            pltpu.VMEM((ROWS, D), BF16),
            pltpu.VMEM((MB, R, hid), BF16),
            pltpu.VMEM((MB, R, hid), BF16),
            pltpu.VMEM((MB, R, hid), BF16),
            pltpu.VMEM((MB, R, hid), F32),
            pltpu.VMEM((MB, R, hid), F32),
            pltpu.VMEM((D, TP * 128), BF16),
            pltpu.VMEM((MB, R, D), BF16),
            pltpu.VMEM((MB, R, D), BF16),
            pltpu.VMEM((MB, C, D), BF16),
            pltpu.VMEM((MB, C, D), BF16),
            pltpu.VMEM((MB, R, D), BF16),
            pltpu.VMEM((MB, R, D), BF16),
            pltpu.VMEM((MB, NX, C, D), BF16),
            pltpu.VMEM((MB, NX, C, D), BF16),
            pltpu.VMEM((MB, C, D), BF16),
            pltpu.VMEM((MB, C, D), BF16),
            pltpu.VMEM((MB, 2, C, D), BF16),
            pltpu.VMEM((MB, 2, C, D), BF16),
            pltpu.VMEM((MB, TP, C, 128), BF16),
            pltpu.VMEM((MB, TP, C, 128), BF16),
            pltpu.VMEM((2, MB, NX, C, 128), BF16),
            pltpu.VMEM((2, MB, NX, C, 128), BF16),
            pltpu.VMEM((MB, TP, R, 128), BF16),
            pltpu.VMEM((TP, MB, R, 128), BF16),
            dma((9,)),
            dma((4,)),
            dma((2, TP)),
            dma((2, TP)),
            dma((2, MB, NX)),
            dma((2, MB, NX)),
            dma((2, MB, NX)),
            dma((2, MB, NX)),
            dma((2, MB, 2)),
            dma((2, MB, 2)),
            dma((2, MB, TP)),
            dma((2, MB, TP)),
        ],
        compiler_params=pltpu.CompilerParams(
            collective_id=0, has_side_effects=True, vmem_limit_bytes=56 * 1024 * 1024
        ),
        name="chain",
    )(acts, cot, *weights, *firsts, *seconds)


def mean(own, other):
    return ((own.astype(F32) + other.astype(F32)) * 0.5).astype(BF16)


def mean_down_kernel(part, rest, rest_moved, *moved_and_out):
    *moved, out = moved_and_out
    moved = [way[...].astype(F32) for way in moved]
    out[:RELAYED, :] = ((part[...].astype(F32) + sum(moved)) * 0.5).astype(BF16)
    out[RELAYED:, :] = mean(rest[...], rest_moved[...])


def mean_down(part, rest, rest_moved, *moved):
    vm = pl.BlockSpec(memory_space=pltpu.VMEM)
    rows = part.shape[0] + rest.shape[0]
    return pl.pallas_call(
        mean_down_kernel,
        out_shape=jax.ShapeDtypeStruct((rows, D), BF16),
        in_specs=[vm] * (3 + len(moved)),
        out_specs=vm,
        cost_estimate=pl.CostEstimate(flops=2 * rows * D, bytes_accessed=6 * rows * D, transcendentals=0),
        name="mean_down",
    )(part, rest, rest_moved, *moved)


def gossip(gate, up, rest, part, distance):
    peers = lax.axis_size("rep")
    onward = [(i, (i + distance) % peers) for i in range(peers)]
    back = [(i, (i - 2) % peers) for i in range(peers) if distance == 2 or i % 2]
    if distance > 2:
        moved = [lax.ppermute(part, "rep", onward)]
    else:
        moved = lax.ppermute(lax.ppermute(part, "rep", back), "rep", back)
        if distance == 1:
            last = [(i, (i - 3) % peers) for i in range(peers) if i % 2]
            within = [(i, i + 1) for i in range(peers) if i % 2 == 0]
            moved = [lax.ppermute(moved, "rep", last), lax.ppermute(part, "rep", within)]
        else:
            moved = [lax.ppermute(moved, "rep", back)]
    pairs = [(own, lax.ppermute(own, "rep", onward)) for own in (gate, up, rest)]
    new_gate, new_up = (mean(*pair) for pair in pairs[:2])
    new_down = mean_down(part, *pairs[2], *moved)
    return lax.optimization_barrier((new_gate, new_up, new_down))


def on_device(
    acts, cotangent, w_gate, w_up, w_down, m_gate, m_up, m_down, v_gate, v_up, v_down, steps
):
    def by_units(gate, up, down):
        return gate[0, 0].T, up[0, 0].T, down[0, 0]

    y, dx, gate, up, part, rest = chain(
        acts[0].T,
        cotangent[0].T,
        by_units(w_gate, w_up, w_down),
        by_units(m_gate, m_up, m_down),
        by_units(v_gate, v_up, v_down),
    )
    levels = lax.axis_size("rep").bit_length() - 1
    branches = [functools.partial(gossip, distance=2**level) for level in range(levels)]
    new_gate, new_up, new_down = lax.switch(
        steps[0] % levels, branches, gate, up, rest, part
    )
    return (
        y.T[None, None],
        dx.T[None, None],
        new_gate.T[None, None],
        new_up.T[None, None],
        new_down[None, None],
    )


def solution(mesh):
    return jax.shard_map(
        on_device,
        mesh=mesh,
        in_specs=(
            P("rep", None, "tp"),
            P("rep", None, "tp"),
            P("section", "rep", None, "tp"),
            P("section", "rep", None, "tp"),
            P("section", "rep", "tp", None),
            P("section", "rep", None, "tp"),
            P("section", "rep", None, "tp"),
            P("section", "rep", "tp", None),
            P("section", "rep", None, "tp"),
            P("section", "rep", None, "tp"),
            P("section", "rep", "tp", None),
            P("section"),
        ),
        out_specs=(
            P("section", "rep", None, "tp"),
            P("section", "rep", None, "tp"),
            P("section", "rep", None, "tp"),
            P("section", "rep", None, "tp"),
            P("section", "rep", "tp", None),
        ),
        check_vma=False,
    )
```

```python
import functools
import math

import jax
import jax.numpy as jnp
from jax import lax
from jax.experimental import pallas as pl
from jax.experimental.pallas import tpu as pltpu
from jax.sharding import PartitionSpec as P


D = 896
FF = 4864
ROWS = 256
SECTIONS = 4
TP = 8
NX = 4
BLOCK = D // TP
MB = 4
R = ROWS // MB
HALF = ROWS // 2
RELAYED = 448
C = R // NX

NORM_EPS = 1e-06
ADAM_EPS = 1e-08
LEARN = 0.3
BETA_ONE = 0.9
BETA_TWO = 0.95
INV_D = 1.0 / math.sqrt(D)
INV_FF = 1.0 / math.sqrt(FF)
MESH = pl.DeviceIdType.MESH
BF16 = jnp.bfloat16
F32 = jnp.float32

CODES = {name: number for number, name in enumerate("IHMThmtOoDGU-")}


PER_WORD = 5


def plan(text):
    return [CODES[name] * MB + int(mb) for name, mb in zip(text[::2], text[1::2])]


def packed(steps):
    words = [steps[at : at + PER_WORD] for at in range(0, len(steps), PER_WORD)]
    return [sum(step << (6 * place) for place, step in enumerate(word)) for word in words]


START = "I0H0H1M0I1H2M1H3T0M2T1M3T2T3"
RETURN = "O0O1O2O3h0h1m0h2m1h3t0m2t1m3t2"
FIRST = plan(START + "O0O1O2O3h0h1m0h2m1h3m2m3D0G0U0")
MIDDLE = plan(START + RETURN + "t3o0o1o2o3D0G0U0")
FIRST = FIRST + plan("-0") * (len(MIDDLE) - len(FIRST))
TURN = plan("I0I1H0H1M0m0H2M1m1t0H3M2m2t1M3m3t2t3")
LAST = TURN + plan("D0G0U0T0T1T2T3O0O1O2O3o0o1o2o3")
LAST = LAST + plan("-0") * (len(MIDDLE) - len(LAST))


def rms_parts(rows):
    xf = rows.astype(F32)
    rms = jnp.sqrt(jnp.mean(xf * xf, axis=1, keepdims=True) + NORM_EPS)
    return xf, rms


def dot_nn(left, right):
    return lax.dot_general(left, right, (((1,), (0,)), ((), ())), preferred_element_type=F32)


def dot_tn(left, right):
    return lax.dot_general(left, right, (((0,), (0,)), ((), ())), preferred_element_type=F32)


def dot_nt(left, right):
    return lax.dot_general(left, right, (((1,), (1,)), ((), ())), preferred_element_type=F32)


def chain_kernel(
    acts,
    cot,
    wg_hbm,
    wu_hbm,
    wd_hbm,
    mg_hbm,
    mu_hbm,
    md_hbm,
    vg_hbm,
    vu_hbm,
    vd_hbm,
    out_y,
    out_dx,
    out_gate,
    out_up,
    out_part,
    out_rest,
    wg,
    wu,
    wd,
    mg,
    mu,
    md,
    vg,
    vu,
    vd,
    ng,
    nu,
    nd,
    grad,
    xin,
    full,
    hidden_s,
    dgate_s,
    dup_s,
    act_s,
    slope_s,
    spread,
    nb,
    dyb,
    xrow,
    dyrow,
    part_f,
    part_b,
    rs_f,
    rs_b,
    zsend_f,
    zsend_b,
    zrecv_f,
    zrecv_b,
    ost_f,
    ost_b,
    orecv_f,
    orecv_b,
    ost_x,
    orecv_x,
    load_sem,
    store_sem,
    in_send,
    in_recv,
    ag_send,
    ag_recv,
    rs_send,
    rs_recv,
    z_send,
    z_recv,
    o_send,
    o_recv,
):
    s = lax.axis_index("section")
    t = lax.axis_index("tp")
    h = t // NX
    x = t % NX
    own = pl.ds(pl.multiple_of(x * C, C), C)

    def peer_x(k):
        return (x + k) % NX

    loads = [
        pltpu.make_async_copy(src, dst, load_sem.at[number])
        for number, (src, dst) in enumerate(
            (
                (wg_hbm, wg),
                (wu_hbm, wu),
                (wd_hbm, wd),
                (md_hbm, md),
                (vd_hbm, vd),
                (mg_hbm, mg),
                (vg_hbm, vg),
                (mu_hbm, mu),
                (vu_hbm, vu),
            )
        )
    ]
    stores = [
        pltpu.make_async_copy(src, dst, store_sem.at[number])
        for number, (src, dst) in enumerate(
            (
                (nd.at[:RELAYED], out_part),
                (nd.at[RELAYED:], out_rest),
                (ng, out_gate),
                (nu, out_up),
            )
        )
    ]
    for load in loads[:3]:
        load.start()

    barrier = pltpu.get_barrier_semaphore()
    for k in range(1, TP):
        pl.semaphore_signal(barrier, inc=1, device_id={"tp": (t + k) % TP}, device_id_type=MESH)
    for step in (1, SECTIONS - 1):
        for hh in range(2):
            pl.semaphore_signal(
                barrier,
                inc=1,
                device_id={"section": (s + step) % SECTIONS, "tp": hh * NX + x},
                device_id_type=MESH,
            )
    pl.semaphore_wait(barrier, TP - 1 + 4)

    def block_of(who):
        return pl.ds(pl.multiple_of(who * BLOCK, BLOCK), BLOCK)

    def half_of(piece):
        return pl.ds(pl.multiple_of(piece * HALF, HALF), HALF)

    def in_copy(src, piece, k):
        return pltpu.make_async_remote_copy(
            src_ref=src.at[:, half_of(piece)],
            dst_ref=xin.at[block_of(t), half_of(piece)],
            send_sem=in_send.at[piece, k],
            recv_sem=in_recv.at[piece, t],
            device_id={"tp": (t + k) % TP},
            device_id_type=MESH,
        )

    def in_wait(piece, k):
        who = (t + k) % TP
        pltpu.make_async_remote_copy(
            src_ref=xin.at[block_of(who), half_of(piece)],
            dst_ref=xin.at[block_of(who), half_of(piece)],
            send_sem=in_send.at[piece, k],
            recv_sem=in_recv.at[piece, who],
            device_id={"tp": who},
            device_id_type=MESH,
        ).wait_recv()

    order = (4, 5, 3, 6, 2, 7, 1)

    @pl.when(s == 0)
    def _():
        for piece in range(2):
            for k in order:
                in_copy(acts, piece, k).start()

    @pl.when(s == SECTIONS - 1)
    def _():
        for piece in range(2):
            for k in order:
                in_copy(cot, piece, k).start()

    for load in loads[3:]:
        load.start()

    def gather_blocks(src, piece):
        xin[block_of(t), half_of(piece)] = src[:, half_of(piece)]
        for k in range(1, TP):
            in_wait(piece, k)
        full[half_of(piece), :] = xin[:, half_of(piece)].astype(F32).T.astype(BF16)

    def ag_copy(buf, kind, mb, k):
        return pltpu.make_async_remote_copy(
            src_ref=buf.at[mb, own],
            dst_ref=buf.at[mb, own],
            send_sem=ag_send.at[kind, mb, k],
            recv_sem=ag_recv.at[kind, mb, NX - k],
            device_id={"tp": h * NX + peer_x(k)},
            device_id_type=MESH,
        )

    def ag_wait(buf, kind, mb, k):
        rows = pl.ds(pl.multiple_of(peer_x(k) * C, C), C)
        pltpu.make_async_remote_copy(
            src_ref=buf.at[mb, rows],
            dst_ref=buf.at[mb, rows],
            send_sem=ag_send.at[kind, mb, k],
            recv_sem=ag_recv.at[kind, mb, k],
            device_id={"tp": h * NX + peer_x(k)},
            device_id_type=MESH,
        ).wait_recv()

    def rs_copy(part, buf, kind, mb, k):
        rows = pl.ds(pl.multiple_of(peer_x(k) * C, C), C)
        return pltpu.make_async_remote_copy(
            src_ref=part.at[mb, rows],
            dst_ref=buf.at[mb, NX - k],
            send_sem=rs_send.at[kind, mb, k],
            recv_sem=rs_recv.at[kind, mb, NX - k],
            device_id={"tp": h * NX + peer_x(k)},
            device_id_type=MESH,
        )

    def rs_wait(part, buf, kind, mb, k):
        rows = pl.ds(pl.multiple_of(peer_x(k) * C, C), C)
        pltpu.make_async_remote_copy(
            src_ref=part.at[mb, rows],
            dst_ref=buf.at[mb, k],
            send_sem=rs_send.at[kind, mb, k],
            recv_sem=rs_recv.at[kind, mb, k],
            device_id={"tp": h * NX + peer_x(k)},
            device_id_type=MESH,
        ).wait_recv()

    def z_copy(src, buf, kind, mb, hh):
        to = s + 1 if kind == 0 else s - 1
        return pltpu.make_async_remote_copy(
            src_ref=src.at[mb],
            dst_ref=buf.at[mb, h],
            send_sem=z_send.at[kind, mb, hh],
            recv_sem=z_recv.at[kind, mb, h],
            device_id={"section": to % SECTIONS, "tp": hh * NX + x},
            device_id_type=MESH,
        )

    def z_wait(src, buf, kind, mb, hh):
        pltpu.make_async_remote_copy(
            src_ref=src.at[mb],
            dst_ref=buf.at[mb, hh],
            send_sem=z_send.at[kind, mb, hh],
            recv_sem=z_recv.at[kind, mb, hh],
            device_id={"tp": (1 - h) * NX + x},
            device_id_type=MESH,
        ).wait_recv()

    def o_copy(ost, orecv, kind, mb, k):
        who = (t + k) % TP
        return pltpu.make_async_remote_copy(
            src_ref=ost.at[mb, who],
            dst_ref=orecv.at[h, mb, x],
            send_sem=o_send.at[kind, mb, k],
            recv_sem=o_recv.at[kind, mb, TP - k],
            device_id={"tp": who},
            device_id_type=MESH,
        )

    def x_copy(mb, k):
        who = (t + k) % TP
        return pltpu.make_async_remote_copy(
            src_ref=ost_x.at[mb, who],
            dst_ref=orecv_x.at[t, mb],
            send_sem=o_send.at[1, mb, k],
            recv_sem=o_recv.at[1, mb, TP - k],
            device_id={"tp": who},
            device_id_type=MESH,
        )

    def x_wait(mb, k):
        who = (t + k) % TP
        pltpu.make_async_remote_copy(
            src_ref=ost_x.at[mb, who],
            dst_ref=orecv_x.at[who, mb],
            send_sem=o_send.at[1, mb, k],
            recv_sem=o_recv.at[1, mb, k],
            device_id={"tp": who},
            device_id_type=MESH,
        ).wait_recv()

    def o_wait(ost, orecv, kind, mb, k):
        who = (t + k) % TP
        pltpu.make_async_remote_copy(
            src_ref=ost.at[mb, who],
            dst_ref=orecv.at[who // NX, mb, who % NX],
            send_sem=o_send.at[kind, mb, k],
            recv_sem=o_recv.at[kind, mb, k],
            device_id={"tp": who},
            device_id_type=MESH,
        ).wait_recv()

    far_first = (2, 1, 3)

    def step_first(piece):
        @pl.when(piece == 0)
        def _():
            for load in loads[:3]:
                load.wait()

        @pl.when(s == 0)
        def _():
            gather_blocks(acts, piece)
            for b in range(MB // 2):
                mb = piece * (MB // 2) + b
                xf, rms = rms_parts(full[pl.ds(pl.multiple_of(mb * R, R), R), :])
                nb[mb] = (xf / rms).astype(BF16)
                xrow[mb] = full[pl.ds(pl.multiple_of(mb * R + x * C, C), C), :]

        @pl.when(s == SECTIONS - 1)
        def _():
            gather_blocks(cot, piece)
            for b in range(MB // 2):
                mb = piece * (MB // 2) + b
                dyb[mb] = full[pl.ds(pl.multiple_of(mb * R, R), R), :]
                dyrow[mb] = full[pl.ds(pl.multiple_of(mb * R + x * C, C), C), :]

    def head_fwd(mb):
        @pl.when(s > 0)
        def _():
            z_wait(zsend_f, zrecv_f, 0, mb, 0)
            z_wait(zsend_f, zrecv_f, 0, mb, 1)
            rows = (zrecv_f[mb, 0].astype(F32) + zrecv_f[mb, 1].astype(F32)).astype(BF16)
            xrow[mb] = rows
            xf, rms = rms_parts(rows)
            nb[mb, own] = (xf / rms).astype(BF16)
            for k in far_first:
                ag_copy(nb, 0, mb, k).start()

    def main_fwd(mb):
        @pl.when(s > 0)
        def _():
            for k in (1, 3, 2):
                ag_wait(nb, 0, mb, k)

        normed = nb[mb]
        gate = dot_nt(normed, wg[...]) * INV_D
        upper = dot_nt(normed, wu[...]) * INV_D
        sig = jax.nn.sigmoid(gate)
        active = gate * sig
        hidden = (active * upper).astype(BF16)
        part_f[mb] = (dot_nn(hidden, wd[...]) * INV_FF).astype(BF16)
        for k in far_first:
            rs_copy(part_f, rs_f, 0, mb, k).start()
        hidden_s[mb] = hidden
        act_s[mb] = active
        slope_s[mb] = upper * sig * (1.0 + gate * (1.0 - sig))

    def half_sum(part, buf, kind, mb):
        for k in (1, 3, 2):
            rs_wait(part, buf, kind, mb, k)
        total = part[mb, own].astype(F32)
        for k in range(1, NX):
            total = total + buf[mb, k].astype(F32)
        return total

    def tail_fwd(mb):
        half = half_sum(part_f, rs_f, 0, mb)
        zsend_f[mb] = (half + 0.5 * xrow[mb].astype(F32)).astype(BF16)

        @pl.when(s < SECTIONS - 1)
        def _():
            z_copy(zsend_f, zrecv_f, 0, mb, 0).start()
            z_copy(zsend_f, zrecv_f, 0, mb, 1).start()

    def head_bwd(mb):
        @pl.when(s < SECTIONS - 1)
        def _():
            z_wait(zsend_b, zrecv_b, 1, mb, 0)
            z_wait(zsend_b, zrecv_b, 1, mb, 1)
            rows = (zrecv_b[mb, 0].astype(F32) + zrecv_b[mb, 1].astype(F32)).astype(BF16)
            dyrow[mb] = rows
            dyb[mb, own] = rows
            for k in far_first:
                ag_copy(dyb, 1, mb, k).start()

    def main_bwd(mb):
        @pl.when(s < SECTIONS - 1)
        def _():
            for k in (1, 3, 2):
                ag_wait(dyb, 1, mb, k)

        dh = dot_nt(dyb[mb], wd[...]) * INV_FF
        dgate = (dh * slope_s[mb]).astype(BF16)
        dup = (dh * act_s[mb]).astype(BF16)
        part = (dot_nn(dgate, wg[...]) + dot_nn(dup, wu[...])) * INV_D

        @pl.when(s > 0)
        def _():
            part_b[mb] = part.astype(BF16)
            for k in far_first:
                rs_copy(part_b, rs_b, 1, mb, k).start()

        @pl.when(s == 0)
        def _():
            xf, rms = rms_parts(full[pl.ds(pl.multiple_of(mb * R, R), R), :])
            normed = xf / rms
            stat = jnp.sum(part * normed, axis=1, keepdims=True) / D
            share = dyb[mb].astype(F32) * (1.0 / TP) + (part - normed * stat) / rms
            wide = dot_nn(share.astype(BF16), spread[...]).astype(BF16)
            for q in range(TP):
                ost_x[mb, q] = wide[:, q * 128 : (q + 1) * 128]
            orecv_x[t, mb] = ost_x[mb, t]
            for k in order:
                x_copy(mb, k).start()

        dgate_s[mb] = dgate
        dup_s[mb] = dup

    def tail_bwd(mb):
        xf, rms = rms_parts(xrow[mb])
        normed = xf / rms
        half = half_sum(part_b, rs_b, 1, mb)
        stat = jnp.sum(half * normed, axis=1, keepdims=True) / D
        grad = 0.5 * dyrow[mb].astype(F32) + (half - normed * stat) / rms
        zsend_b[mb] = grad.astype(BF16)

        z_copy(zsend_b, zrecv_b, 1, mb, 0).start()
        z_copy(zsend_b, zrecv_b, 1, mb, 1).start()

    def spread_columns(zsend, ost, orecv, kind, mb):
        wide = dot_nn(zsend[mb], spread[...]).astype(BF16)
        for q in range(TP):
            ost[mb, q] = wide[:, q * 128 : (q + 1) * 128]
        orecv[h, mb, x] = ost[mb, t]
        for k in order:
            o_copy(ost, orecv, kind, mb, k).start()

    def out_fwd(mb):
        @pl.when(mb == 0)
        def _():
            feature = lax.broadcasted_iota(jnp.int32, (D, TP * 128), 0)
            place = lax.broadcasted_iota(jnp.int32, (D, TP * 128), 1)
            lane = place % 128
            hit = (feature == (place // 128) * BLOCK + lane) & (lane < BLOCK)
            spread[...] = jnp.where(hit, 1.0, 0.0).astype(BF16)

        spread_columns(zsend_f, ost_f, orecv_f, 0, mb)

    def out_bwd(mb):
        spread_columns(zsend_b, ost_b, orecv_b, 1, mb)

    def update(number, units, rows, scale, weight, first, second, new):
        loads[3 + 2 * number].wait()
        loads[4 + 2 * number].wait()
        hid = weight.shape[0]
        grad[...] = dot_tn(units[...].reshape(ROWS, hid), rows[...].reshape(ROWS, D)) * scale

        def piece(index, carry):
            part = pl.ds(pl.multiple_of(index * 32, 32), 32)
            g = grad[part, :]
            m_new = BETA_ONE * first[part, :].astype(F32) + (1.0 - BETA_ONE) * g
            v_new = BETA_TWO * second[part, :].astype(F32) + (1.0 - BETA_TWO) * g * g
            step = LEARN * m_new / (jnp.sqrt(v_new) + ADAM_EPS)
            new[part, :] = (weight[part, :].astype(F32) - step).astype(BF16)
            return carry

        lax.fori_loop(0, hid // 32, piece, 0)
        for store in stores[:2] if number == 0 else stores[number + 1 : number + 2]:
            store.start()

    def update_down(mb):
        update(0, hidden_s, dyb, INV_FF, wd, md, vd, nd)

    def update_gate(mb):
        update(1, dgate_s, nb, INV_D, wg, mg, vg, ng)

    def update_up(mb):
        update(2, dup_s, nb, INV_D, wu, mu, vu, nu)

    def finish():
        def columns(kind, ost, orecv, out):
            for b in range(MB):
                for k in range(1, TP):
                    o_wait(ost, orecv, kind, b, k)
            halves = orecv[...].reshape(2, ROWS, 128).astype(F32)
            out[...] = (halves[0] + halves[1]).T[:BLOCK].astype(BF16)

        columns(0, ost_f, orecv_f, out_y)

        @pl.when(s > 0)
        def _():
            columns(1, ost_b, orecv_b, out_dx)

        @pl.when(s == 0)
        def _():
            for b in range(MB):
                for k in range(1, TP):
                    x_wait(b, k)
            total = orecv_x[0].reshape(ROWS, 128).astype(F32)
            for q in range(1, TP):
                total = total + orecv_x[q].reshape(ROWS, 128).astype(F32)
            out_dx[...] = total.T[:BLOCK].astype(BF16)

    steps = (
        step_first,
        head_fwd,
        main_fwd,
        tail_fwd,
        head_bwd,
        main_bwd,
        tail_bwd,
        out_fwd,
        out_bwd,
        update_down,
        update_gate,
        update_up,
        lambda mb: None,
    )

    words = [
        jnp.where(s == 0, first, jnp.where(s == SECTIONS - 1, last, middle))
        for first, middle, last in zip(packed(FIRST), packed(MIDDLE), packed(LAST))
    ]

    def run(index, carry):
        word = words[0]
        for place in range(1, len(words)):
            word = jnp.where(index // PER_WORD == place, words[place], word)
        step = (word >> (6 * (index % PER_WORD))) & 63
        mb = step % MB
        code = step // MB

        def dispatch(low, high):
            if high - low == 1:
                steps[low](mb)
                return
            middle = (low + high) // 2

            @pl.when(code < middle)
            def _():
                dispatch(low, middle)

            @pl.when(code >= middle)
            def _():
                dispatch(middle, high)

        dispatch(0, len(steps))
        return carry

    lax.fori_loop(0, len(MIDDLE), run, 0)

    for store in stores:
        store.wait()

    @pl.when(s == 0)
    def _():
        for piece in range(2):
            for k in order:
                in_copy(acts, piece, k).wait_send()

    @pl.when(s == SECTIONS - 1)
    def _():
        for piece in range(2):
            for k in order:
                in_copy(cot, piece, k).wait_send()

    def drain(mb, carry):
        for k in far_first:
            rs_copy(part_f, rs_f, 0, mb, k).wait_send()
        for k in range(1, TP):
            o_copy(ost_f, orecv_f, 0, mb, k).wait_send()

        @pl.when(s == 0)
        def _():
            for k in range(1, TP):
                x_copy(mb, k).wait_send()

        @pl.when(s > 0)
        def _():
            for k in far_first:
                ag_copy(nb, 0, mb, k).wait_send()
                rs_copy(part_b, rs_b, 1, mb, k).wait_send()
            for k in range(1, TP):
                o_copy(ost_b, orecv_b, 1, mb, k).wait_send()
            for hh in range(2):
                z_copy(zsend_b, zrecv_b, 1, mb, hh).wait_send()

        @pl.when(s < SECTIONS - 1)
        def _():
            for k in far_first:
                ag_copy(dyb, 1, mb, k).wait_send()
            for hh in range(2):
                z_copy(zsend_f, zrecv_f, 0, mb, hh).wait_send()

        return carry

    lax.fori_loop(0, MB, drain, 0)
    finish()


def chain(acts, cot, weights, firsts, seconds):
    hid = weights[0].shape[0]
    vm = pl.BlockSpec(memory_space=pltpu.VMEM)
    hbm = pl.BlockSpec(memory_space=pl.ANY)
    shape = jax.ShapeDtypeStruct
    dma = pltpu.SemaphoreType.DMA
    return pl.pallas_call(
        chain_kernel,
        out_shape=(shape((BLOCK, ROWS), BF16),) * 2
        + (shape((hid, D), BF16),) * 2
        + (shape((RELAYED, D), BF16), shape((hid - RELAYED, D), BF16)),
        in_specs=[vm] * 2 + [hbm] * 9,
        out_specs=[vm] * 2 + [hbm] * 4,
        scratch_shapes=[pltpu.VMEM((hid, D), BF16)] * 12
        + [
            pltpu.VMEM((hid, D), F32),
            pltpu.VMEM((D, ROWS), BF16),
            pltpu.VMEM((ROWS, D), BF16),
            pltpu.VMEM((MB, R, hid), BF16),
            pltpu.VMEM((MB, R, hid), BF16),
            pltpu.VMEM((MB, R, hid), BF16),
            pltpu.VMEM((MB, R, hid), F32),
            pltpu.VMEM((MB, R, hid), F32),
            pltpu.VMEM((D, TP * 128), BF16),
            pltpu.VMEM((MB, R, D), BF16),
            pltpu.VMEM((MB, R, D), BF16),
            pltpu.VMEM((MB, C, D), BF16),
            pltpu.VMEM((MB, C, D), BF16),
            pltpu.VMEM((MB, R, D), BF16),
            pltpu.VMEM((MB, R, D), BF16),
            pltpu.VMEM((MB, NX, C, D), BF16),
            pltpu.VMEM((MB, NX, C, D), BF16),
            pltpu.VMEM((MB, C, D), BF16),
            pltpu.VMEM((MB, C, D), BF16),
            pltpu.VMEM((MB, 2, C, D), BF16),
            pltpu.VMEM((MB, 2, C, D), BF16),
            pltpu.VMEM((MB, TP, C, 128), BF16),
            pltpu.VMEM((MB, TP, C, 128), BF16),
            pltpu.VMEM((2, MB, NX, C, 128), BF16),
            pltpu.VMEM((2, MB, NX, C, 128), BF16),
            pltpu.VMEM((MB, TP, R, 128), BF16),
            pltpu.VMEM((TP, MB, R, 128), BF16),
            dma((9,)),
            dma((4,)),
            dma((2, TP)),
            dma((2, TP)),
            dma((2, MB, NX)),
            dma((2, MB, NX)),
            dma((2, MB, NX)),
            dma((2, MB, NX)),
            dma((2, MB, 2)),
            dma((2, MB, 2)),
            dma((2, MB, TP)),
            dma((2, MB, TP)),
        ],
        compiler_params=pltpu.CompilerParams(
            collective_id=0, has_side_effects=True, vmem_limit_bytes=56 * 1024 * 1024
        ),
        name="chain",
    )(acts, cot, *weights, *firsts, *seconds)


def mean(own, other):
    return ((own.astype(F32) + other.astype(F32)) * 0.5).astype(BF16)


def mean_down_kernel(part, rest, rest_moved, *moved_and_out):
    *moved, out = moved_and_out
    moved = [way[...].astype(F32) for way in moved]
    out[:RELAYED, :] = ((part[...].astype(F32) + sum(moved)) * 0.5).astype(BF16)
    out[RELAYED:, :] = mean(rest[...], rest_moved[...])


def mean_down(part, rest, rest_moved, *moved):
    vm = pl.BlockSpec(memory_space=pltpu.VMEM)
    rows = part.shape[0] + rest.shape[0]
    return pl.pallas_call(
        mean_down_kernel,
        out_shape=jax.ShapeDtypeStruct((rows, D), BF16),
        in_specs=[vm] * (3 + len(moved)),
        out_specs=vm,
        cost_estimate=pl.CostEstimate(flops=2 * rows * D, bytes_accessed=6 * rows * D, transcendentals=0),
        name="mean_down",
    )(part, rest, rest_moved, *moved)


def gossip(gate, up, rest, part, distance):
    peers = lax.axis_size("rep")
    onward = [(i, (i + distance) % peers) for i in range(peers)]
    back = [(i, (i - 2) % peers) for i in range(peers) if distance == 2 or i % 2]
    if distance > 2:
        moved = [lax.ppermute(part, "rep", onward)]
    else:
        moved = lax.ppermute(part, "rep", back)
        moved = lax.ppermute(moved, "rep", back)
        if distance == 1:
            last = [(i, (i - 3) % peers) for i in range(peers) if i % 2]
            within = [(i, i + 1) for i in range(peers) if i % 2 == 0]
            moved = [lax.ppermute(moved, "rep", last), lax.ppermute(part, "rep", within)]
        else:
            moved = [lax.ppermute(moved, "rep", back)]
    pairs = []
    for own in (gate, rest, up):
        pairs.append((own, lax.ppermute(own, "rep", onward)))
    new_gate, new_up = mean(*pairs[0]), mean(*pairs[2])
    new_down = mean_down(part, *pairs[1], *moved)
    return lax.optimization_barrier((new_gate, new_up, new_down))


def on_device(
    acts, cotangent, w_gate, w_up, w_down, m_gate, m_up, m_down, v_gate, v_up, v_down, steps
):
    def by_units(gate, up, down):
        return gate[0, 0].T, up[0, 0].T, down[0, 0]

    y, dx, gate, up, part, rest = chain(
        acts[0].T,
        cotangent[0].T,
        by_units(w_gate, w_up, w_down),
        by_units(m_gate, m_up, m_down),
        by_units(v_gate, v_up, v_down),
    )
    levels = lax.axis_size("rep").bit_length() - 1
    branches = [functools.partial(gossip, distance=2**level) for level in range(levels)]
    new_gate, new_up, new_down = lax.switch(
        steps[0] % levels, branches, gate, up, rest, part
    )
    return (
        y.T[None, None],
        dx.T[None, None],
        new_gate.T[None, None],
        new_up.T[None, None],
        new_down[None, None],
    )


def solution(mesh):
    return jax.shard_map(
        on_device,
        mesh=mesh,
        in_specs=(
            P("rep", None, "tp"),
            P("rep", None, "tp"),
            P("section", "rep", None, "tp"),
            P("section", "rep", None, "tp"),
            P("section", "rep", "tp", None),
            P("section", "rep", None, "tp"),
            P("section", "rep", None, "tp"),
            P("section", "rep", "tp", None),
            P("section", "rep", None, "tp"),
            P("section", "rep", None, "tp"),
            P("section", "rep", "tp", None),
            P("section"),
        ),
        out_specs=(
            P("section", "rep", None, "tp"),
            P("section", "rep", None, "tp"),
            P("section", "rep", None, "tp"),
            P("section", "rep", None, "tp"),
            P("section", "rep", "tp", None),
        ),
        check_vma=False,
    )
```

```python
import functools
import math

import jax
import jax.numpy as jnp
from jax import lax
from jax.experimental import pallas as pl
from jax.experimental.pallas import tpu as pltpu
from jax.sharding import PartitionSpec as P


D = 896
FF = 4864
ROWS = 256
SECTIONS = 4
TP = 8
NX = 4
BLOCK = D // TP
MB = 4
R = ROWS // MB
HALF = ROWS // 2
RELAYED = 416
C = R // NX

NORM_EPS = 1e-06
ADAM_EPS = 1e-08
LEARN = 0.3
BETA_ONE = 0.9
BETA_TWO = 0.95
INV_D = 1.0 / math.sqrt(D)
INV_FF = 1.0 / math.sqrt(FF)
MESH = pl.DeviceIdType.MESH
BF16 = jnp.bfloat16
F32 = jnp.float32

CODES = {name: number for number, name in enumerate("IHMThmtOoDGU-")}


PER_WORD = 5


def plan(text):
    return [CODES[name] * MB + int(mb) for name, mb in zip(text[::2], text[1::2])]


def packed(steps):
    words = [steps[at : at + PER_WORD] for at in range(0, len(steps), PER_WORD)]
    return [sum(step << (6 * place) for place, step in enumerate(word)) for word in words]


START = "I0H0H1M0I1H2M1H3T0M2T1M3T2T3"
RETURN = "O0O1O2O3h0h1m0h2m1h3t0m2t1m3t2"
FIRST = plan(START + "O0O1O2O3h0h1m0h2m1h3m2m3D0G0U0")
MIDDLE = plan(START + RETURN + "t3o0o1o2o3D0G0U0")
FIRST = FIRST + plan("-0") * (len(MIDDLE) - len(FIRST))
TURN = plan("I0I1H0H1M0m0H2M1m1t0H3M2m2t1M3m3t2t3")
LAST = TURN + plan("D0G0U0T0T1T2T3O0O1O2O3o0o1o2o3")
LAST = LAST + plan("-0") * (len(MIDDLE) - len(LAST))


def rms_parts(rows):
    xf = rows.astype(F32)
    rms = jnp.sqrt(jnp.mean(xf * xf, axis=1, keepdims=True) + NORM_EPS)
    return xf, rms


def dot_nn(left, right):
    return lax.dot_general(left, right, (((1,), (0,)), ((), ())), preferred_element_type=F32)


def dot_tn(left, right):
    return lax.dot_general(left, right, (((0,), (0,)), ((), ())), preferred_element_type=F32)


def dot_nt(left, right):
    return lax.dot_general(left, right, (((1,), (1,)), ((), ())), preferred_element_type=F32)


def chain_kernel(
    acts,
    cot,
    wg_hbm,
    wu_hbm,
    wd_hbm,
    mg_hbm,
    mu_hbm,
    md_hbm,
    vg_hbm,
    vu_hbm,
    vd_hbm,
    out_y,
    out_dx,
    out_gate,
    out_up,
    out_part,
    out_rest,
    wg,
    wu,
    wd,
    mg,
    mu,
    md,
    vg,
    vu,
    vd,
    ng,
    nu,
    nd,
    grad,
    xin,
    full,
    hidden_s,
    dgate_s,
    dup_s,
    act_s,
    slope_s,
    spread,
    nb,
    dyb,
    xrow,
    dyrow,
    part_f,
    part_b,
    rs_f,
    rs_b,
    zsend_f,
    zsend_b,
    zrecv_f,
    zrecv_b,
    ost_f,
    ost_b,
    orecv_f,
    orecv_b,
    ost_x,
    orecv_x,
    load_sem,
    store_sem,
    in_send,
    in_recv,
    ag_send,
    ag_recv,
    rs_send,
    rs_recv,
    z_send,
    z_recv,
    o_send,
    o_recv,
):
    s = lax.axis_index("section")
    t = lax.axis_index("tp")
    h = t // NX
    x = t % NX
    own = pl.ds(pl.multiple_of(x * C, C), C)

    def peer_x(k):
        return (x + k) % NX

    loads = [
        pltpu.make_async_copy(src, dst, load_sem.at[number])
        for number, (src, dst) in enumerate(
            (
                (wg_hbm, wg),
                (wu_hbm, wu),
                (wd_hbm, wd),
                (md_hbm, md),
                (vd_hbm, vd),
                (mg_hbm, mg),
                (vg_hbm, vg),
                (mu_hbm, mu),
                (vu_hbm, vu),
            )
        )
    ]
    stores = [
        pltpu.make_async_copy(src, dst, store_sem.at[number])
        for number, (src, dst) in enumerate(
            (
                (nd.at[:RELAYED], out_part),
                (nd.at[RELAYED:], out_rest),
                (ng, out_gate),
                (nu, out_up),
            )
        )
    ]
    for load in loads[:3]:
        load.start()

    barrier = pltpu.get_barrier_semaphore()
    for k in range(1, TP):
        pl.semaphore_signal(barrier, inc=1, device_id={"tp": (t + k) % TP}, device_id_type=MESH)
    for step in (1, SECTIONS - 1):
        for hh in range(2):
            pl.semaphore_signal(
                barrier,
                inc=1,
                device_id={"section": (s + step) % SECTIONS, "tp": hh * NX + x},
                device_id_type=MESH,
            )
    pl.semaphore_wait(barrier, TP - 1 + 4)

    def block_of(who):
        return pl.ds(pl.multiple_of(who * BLOCK, BLOCK), BLOCK)

    def half_of(piece):
        return pl.ds(pl.multiple_of(piece * HALF, HALF), HALF)

    def in_copy(src, piece, k):
        return pltpu.make_async_remote_copy(
            src_ref=src.at[:, half_of(piece)],
            dst_ref=xin.at[block_of(t), half_of(piece)],
            send_sem=in_send.at[piece, k],
            recv_sem=in_recv.at[piece, t],
            device_id={"tp": (t + k) % TP},
            device_id_type=MESH,
        )

    def in_wait(piece, k):
        who = (t + k) % TP
        pltpu.make_async_remote_copy(
            src_ref=xin.at[block_of(who), half_of(piece)],
            dst_ref=xin.at[block_of(who), half_of(piece)],
            send_sem=in_send.at[piece, k],
            recv_sem=in_recv.at[piece, who],
            device_id={"tp": who},
            device_id_type=MESH,
        ).wait_recv()

    order = (4, 5, 3, 6, 2, 7, 1)

    @pl.when(s == 0)
    def _():
        for piece in range(2):
            for k in order:
                in_copy(acts, piece, k).start()

    @pl.when(s == SECTIONS - 1)
    def _():
        for piece in range(2):
            for k in order:
                in_copy(cot, piece, k).start()

    for load in loads[3:]:
        load.start()

    def gather_blocks(src, piece):
        xin[block_of(t), half_of(piece)] = src[:, half_of(piece)]
        for k in range(1, TP):
            in_wait(piece, k)
        full[half_of(piece), :] = xin[:, half_of(piece)].astype(F32).T.astype(BF16)

    def ag_copy(buf, kind, mb, k):
        return pltpu.make_async_remote_copy(
            src_ref=buf.at[mb, own],
            dst_ref=buf.at[mb, own],
            send_sem=ag_send.at[kind, mb, k],
            recv_sem=ag_recv.at[kind, mb, NX - k],
            device_id={"tp": h * NX + peer_x(k)},
            device_id_type=MESH,
        )

    def ag_wait(buf, kind, mb, k):
        rows = pl.ds(pl.multiple_of(peer_x(k) * C, C), C)
        pltpu.make_async_remote_copy(
            src_ref=buf.at[mb, rows],
            dst_ref=buf.at[mb, rows],
            send_sem=ag_send.at[kind, mb, k],
            recv_sem=ag_recv.at[kind, mb, k],
            device_id={"tp": h * NX + peer_x(k)},
            device_id_type=MESH,
        ).wait_recv()

    def rs_copy(part, buf, kind, mb, k):
        rows = pl.ds(pl.multiple_of(peer_x(k) * C, C), C)
        return pltpu.make_async_remote_copy(
            src_ref=part.at[mb, rows],
            dst_ref=buf.at[mb, NX - k],
            send_sem=rs_send.at[kind, mb, k],
            recv_sem=rs_recv.at[kind, mb, NX - k],
            device_id={"tp": h * NX + peer_x(k)},
            device_id_type=MESH,
        )

    def rs_wait(part, buf, kind, mb, k):
        rows = pl.ds(pl.multiple_of(peer_x(k) * C, C), C)
        pltpu.make_async_remote_copy(
            src_ref=part.at[mb, rows],
            dst_ref=buf.at[mb, k],
            send_sem=rs_send.at[kind, mb, k],
            recv_sem=rs_recv.at[kind, mb, k],
            device_id={"tp": h * NX + peer_x(k)},
            device_id_type=MESH,
        ).wait_recv()

    def z_copy(src, buf, kind, mb, hh):
        to = s + 1 if kind == 0 else s - 1
        return pltpu.make_async_remote_copy(
            src_ref=src.at[mb],
            dst_ref=buf.at[mb, h],
            send_sem=z_send.at[kind, mb, hh],
            recv_sem=z_recv.at[kind, mb, h],
            device_id={"section": to % SECTIONS, "tp": hh * NX + x},
            device_id_type=MESH,
        )

    def z_wait(src, buf, kind, mb, hh):
        pltpu.make_async_remote_copy(
            src_ref=src.at[mb],
            dst_ref=buf.at[mb, hh],
            send_sem=z_send.at[kind, mb, hh],
            recv_sem=z_recv.at[kind, mb, hh],
            device_id={"tp": (1 - h) * NX + x},
            device_id_type=MESH,
        ).wait_recv()

    def o_copy(ost, orecv, kind, mb, k):
        who = (t + k) % TP
        return pltpu.make_async_remote_copy(
            src_ref=ost.at[mb, who],
            dst_ref=orecv.at[h, mb, x],
            send_sem=o_send.at[kind, mb, k],
            recv_sem=o_recv.at[kind, mb, TP - k],
            device_id={"tp": who},
            device_id_type=MESH,
        )

    def x_copy(mb, k):
        who = (t + k) % TP
        return pltpu.make_async_remote_copy(
            src_ref=ost_x.at[mb, who],
            dst_ref=orecv_x.at[t, mb],
            send_sem=o_send.at[1, mb, k],
            recv_sem=o_recv.at[1, mb, TP - k],
            device_id={"tp": who},
            device_id_type=MESH,
        )

    def x_wait(mb, k):
        who = (t + k) % TP
        pltpu.make_async_remote_copy(
            src_ref=ost_x.at[mb, who],
            dst_ref=orecv_x.at[who, mb],
            send_sem=o_send.at[1, mb, k],
            recv_sem=o_recv.at[1, mb, k],
            device_id={"tp": who},
            device_id_type=MESH,
        ).wait_recv()

    def o_wait(ost, orecv, kind, mb, k):
        who = (t + k) % TP
        pltpu.make_async_remote_copy(
            src_ref=ost.at[mb, who],
            dst_ref=orecv.at[who // NX, mb, who % NX],
            send_sem=o_send.at[kind, mb, k],
            recv_sem=o_recv.at[kind, mb, k],
            device_id={"tp": who},
            device_id_type=MESH,
        ).wait_recv()

    far_first = (2, 1, 3)

    def step_first(piece):
        @pl.when(piece == 0)
        def _():
            for load in loads[:3]:
                load.wait()

        @pl.when(s == 0)
        def _():
            gather_blocks(acts, piece)
            for b in range(MB // 2):
                mb = piece * (MB // 2) + b
                xf, rms = rms_parts(full[pl.ds(pl.multiple_of(mb * R, R), R), :])
                nb[mb] = (xf / rms).astype(BF16)
                xrow[mb] = full[pl.ds(pl.multiple_of(mb * R + x * C, C), C), :]

        @pl.when(s == SECTIONS - 1)
        def _():
            gather_blocks(cot, piece)
            for b in range(MB // 2):
                mb = piece * (MB // 2) + b
                dyb[mb] = full[pl.ds(pl.multiple_of(mb * R, R), R), :]
                dyrow[mb] = full[pl.ds(pl.multiple_of(mb * R + x * C, C), C), :]

    def head_fwd(mb):
        @pl.when(s > 0)
        def _():
            z_wait(zsend_f, zrecv_f, 0, mb, 0)
            z_wait(zsend_f, zrecv_f, 0, mb, 1)
            rows = (zrecv_f[mb, 0].astype(F32) + zrecv_f[mb, 1].astype(F32)).astype(BF16)
            xrow[mb] = rows
            xf, rms = rms_parts(rows)
            nb[mb, own] = (xf / rms).astype(BF16)
            for k in far_first:
                ag_copy(nb, 0, mb, k).start()

    def main_fwd(mb):
        @pl.when(s > 0)
        def _():
            for k in (1, 3, 2):
                ag_wait(nb, 0, mb, k)

        normed = nb[mb]
        gate = dot_nt(normed, wg[...]) * INV_D
        upper = dot_nt(normed, wu[...]) * INV_D
        sig = jax.nn.sigmoid(gate)
        active = gate * sig
        hidden = (active * upper).astype(BF16)
        part_f[mb] = (dot_nn(hidden, wd[...]) * INV_FF).astype(BF16)
        for k in far_first:
            rs_copy(part_f, rs_f, 0, mb, k).start()
        hidden_s[mb] = hidden
        act_s[mb] = active
        slope_s[mb] = upper * sig * (1.0 + gate * (1.0 - sig))

    def half_sum(part, buf, kind, mb):
        for k in (1, 3, 2):
            rs_wait(part, buf, kind, mb, k)
        total = part[mb, own].astype(F32)
        for k in range(1, NX):
            total = total + buf[mb, k].astype(F32)
        return total

    def tail_fwd(mb):
        half = half_sum(part_f, rs_f, 0, mb)
        zsend_f[mb] = (half + 0.5 * xrow[mb].astype(F32)).astype(BF16)

        @pl.when(s < SECTIONS - 1)
        def _():
            z_copy(zsend_f, zrecv_f, 0, mb, 0).start()
            z_copy(zsend_f, zrecv_f, 0, mb, 1).start()

    def head_bwd(mb):
        @pl.when(s < SECTIONS - 1)
        def _():
            z_wait(zsend_b, zrecv_b, 1, mb, 0)
            z_wait(zsend_b, zrecv_b, 1, mb, 1)
            rows = (zrecv_b[mb, 0].astype(F32) + zrecv_b[mb, 1].astype(F32)).astype(BF16)
            dyrow[mb] = rows
            dyb[mb, own] = rows
            for k in far_first:
                ag_copy(dyb, 1, mb, k).start()

    def main_bwd(mb):
        @pl.when(s < SECTIONS - 1)
        def _():
            for k in (1, 3, 2):
                ag_wait(dyb, 1, mb, k)

        dh = dot_nt(dyb[mb], wd[...]) * INV_FF
        dgate = (dh * slope_s[mb]).astype(BF16)
        dup = (dh * act_s[mb]).astype(BF16)
        part = (dot_nn(dgate, wg[...]) + dot_nn(dup, wu[...])) * INV_D

        @pl.when(s > 0)
        def _():
            part_b[mb] = part.astype(BF16)
            for k in far_first:
                rs_copy(part_b, rs_b, 1, mb, k).start()

        @pl.when(s == 0)
        def _():
            xf, rms = rms_parts(full[pl.ds(pl.multiple_of(mb * R, R), R), :])
            normed = xf / rms
            stat = jnp.sum(part * normed, axis=1, keepdims=True) / D
            share = dyb[mb].astype(F32) * (1.0 / TP) + (part - normed * stat) / rms
            wide = dot_nn(share.astype(BF16), spread[...]).astype(BF16)
            for q in range(TP):
                ost_x[mb, q] = wide[:, q * 128 : (q + 1) * 128]
            orecv_x[t, mb] = ost_x[mb, t]
            for k in order:
                x_copy(mb, k).start()

        dgate_s[mb] = dgate
        dup_s[mb] = dup

    def tail_bwd(mb):
        xf, rms = rms_parts(xrow[mb])
        normed = xf / rms
        half = half_sum(part_b, rs_b, 1, mb)
        stat = jnp.sum(half * normed, axis=1, keepdims=True) / D
        grad = 0.5 * dyrow[mb].astype(F32) + (half - normed * stat) / rms
        zsend_b[mb] = grad.astype(BF16)

        z_copy(zsend_b, zrecv_b, 1, mb, 0).start()
        z_copy(zsend_b, zrecv_b, 1, mb, 1).start()

    def spread_columns(zsend, ost, orecv, kind, mb):
        wide = dot_nn(zsend[mb], spread[...]).astype(BF16)
        for q in range(TP):
            ost[mb, q] = wide[:, q * 128 : (q + 1) * 128]
        orecv[h, mb, x] = ost[mb, t]
        for k in order:
            o_copy(ost, orecv, kind, mb, k).start()

    def out_fwd(mb):
        @pl.when(mb == 0)
        def _():
            feature = lax.broadcasted_iota(jnp.int32, (D, TP * 128), 0)
            place = lax.broadcasted_iota(jnp.int32, (D, TP * 128), 1)
            lane = place % 128
            hit = (feature == (place // 128) * BLOCK + lane) & (lane < BLOCK)
            spread[...] = jnp.where(hit, 1.0, 0.0).astype(BF16)

        spread_columns(zsend_f, ost_f, orecv_f, 0, mb)

    def out_bwd(mb):
        spread_columns(zsend_b, ost_b, orecv_b, 1, mb)

    def update(number, units, rows, scale, weight, first, second, new):
        loads[3 + 2 * number].wait()
        loads[4 + 2 * number].wait()
        hid = weight.shape[0]
        grad[...] = dot_tn(units[...].reshape(ROWS, hid), rows[...].reshape(ROWS, D)) * scale

        def piece(index, carry):
            part = pl.ds(pl.multiple_of(index * 32, 32), 32)
            g = grad[part, :]
            m_new = BETA_ONE * first[part, :].astype(F32) + (1.0 - BETA_ONE) * g
            v_new = BETA_TWO * second[part, :].astype(F32) + (1.0 - BETA_TWO) * g * g
            step = LEARN * m_new / (jnp.sqrt(v_new) + ADAM_EPS)
            new[part, :] = (weight[part, :].astype(F32) - step).astype(BF16)
            return carry

        lax.fori_loop(0, hid // 32, piece, 0)
        for store in stores[:2] if number == 0 else stores[number + 1 : number + 2]:
            store.start()

    def update_down(mb):
        update(0, hidden_s, dyb, INV_FF, wd, md, vd, nd)

    def update_gate(mb):
        update(1, dgate_s, nb, INV_D, wg, mg, vg, ng)

    def update_up(mb):
        update(2, dup_s, nb, INV_D, wu, mu, vu, nu)

    def finish():
        def columns(kind, ost, orecv, out):
            for b in range(MB):
                for k in range(1, TP):
                    o_wait(ost, orecv, kind, b, k)
            halves = orecv[...].reshape(2, ROWS, 128).astype(F32)
            out[...] = (halves[0] + halves[1]).T[:BLOCK]

        columns(0, ost_f, orecv_f, out_y)

        @pl.when(s > 0)
        def _():
            columns(1, ost_b, orecv_b, out_dx)

        @pl.when(s == 0)
        def _():
            for b in range(MB):
                for k in range(1, TP):
                    x_wait(b, k)
            total = orecv_x[0].reshape(ROWS, 128).astype(F32)
            for q in range(1, TP):
                total = total + orecv_x[q].reshape(ROWS, 128).astype(F32)
            out_dx[...] = total.T[:BLOCK]

    steps = (
        step_first,
        head_fwd,
        main_fwd,
        tail_fwd,
        head_bwd,
        main_bwd,
        tail_bwd,
        out_fwd,
        out_bwd,
        update_down,
        update_gate,
        update_up,
        lambda mb: None,
    )

    words = [
        jnp.where(s == 0, first, jnp.where(s == SECTIONS - 1, last, middle))
        for first, middle, last in zip(packed(FIRST), packed(MIDDLE), packed(LAST))
    ]

    def run(index, carry):
        word = words[0]
        for place in range(1, len(words)):
            word = jnp.where(index // PER_WORD == place, words[place], word)
        step = (word >> (6 * (index % PER_WORD))) & 63
        mb = step % MB
        code = step // MB

        def dispatch(low, high):
            if high - low == 1:
                steps[low](mb)
                return
            middle = (low + high) // 2

            @pl.when(code < middle)
            def _():
                dispatch(low, middle)

            @pl.when(code >= middle)
            def _():
                dispatch(middle, high)

        dispatch(0, len(steps))
        return carry

    lax.fori_loop(0, len(MIDDLE), run, 0)

    for store in stores:
        store.wait()

    @pl.when(s == 0)
    def _():
        for piece in range(2):
            for k in order:
                in_copy(acts, piece, k).wait_send()

    @pl.when(s == SECTIONS - 1)
    def _():
        for piece in range(2):
            for k in order:
                in_copy(cot, piece, k).wait_send()

    def drain(mb, carry):
        for k in far_first:
            rs_copy(part_f, rs_f, 0, mb, k).wait_send()
        for k in range(1, TP):
            o_copy(ost_f, orecv_f, 0, mb, k).wait_send()

        @pl.when(s == 0)
        def _():
            for k in range(1, TP):
                x_copy(mb, k).wait_send()

        @pl.when(s > 0)
        def _():
            for k in far_first:
                ag_copy(nb, 0, mb, k).wait_send()
                rs_copy(part_b, rs_b, 1, mb, k).wait_send()
            for k in range(1, TP):
                o_copy(ost_b, orecv_b, 1, mb, k).wait_send()
            for hh in range(2):
                z_copy(zsend_b, zrecv_b, 1, mb, hh).wait_send()

        @pl.when(s < SECTIONS - 1)
        def _():
            for k in far_first:
                ag_copy(dyb, 1, mb, k).wait_send()
            for hh in range(2):
                z_copy(zsend_f, zrecv_f, 0, mb, hh).wait_send()

        return carry

    lax.fori_loop(0, MB, drain, 0)
    finish()


def chain(acts, cot, weights, firsts, seconds):
    hid = weights[0].shape[0]
    vm = pl.BlockSpec(memory_space=pltpu.VMEM)
    hbm = pl.BlockSpec(memory_space=pl.ANY)
    shape = jax.ShapeDtypeStruct
    dma = pltpu.SemaphoreType.DMA
    return pl.pallas_call(
        chain_kernel,
        out_shape=(shape((BLOCK, ROWS), F32),) * 2
        + (shape((hid, D), BF16),) * 2
        + (shape((RELAYED, D), BF16), shape((hid - RELAYED, D), BF16)),
        in_specs=[vm] * 2 + [hbm] * 9,
        out_specs=[vm] * 2 + [hbm] * 4,
        scratch_shapes=[pltpu.VMEM((hid, D), BF16)] * 12
        + [
            pltpu.VMEM((hid, D), F32),
            pltpu.VMEM((D, ROWS), BF16),
            pltpu.VMEM((ROWS, D), BF16),
            pltpu.VMEM((MB, R, hid), BF16),
            pltpu.VMEM((MB, R, hid), BF16),
            pltpu.VMEM((MB, R, hid), BF16),
            pltpu.VMEM((MB, R, hid), F32),
            pltpu.VMEM((MB, R, hid), F32),
            pltpu.VMEM((D, TP * 128), BF16),
            pltpu.VMEM((MB, R, D), BF16),
            pltpu.VMEM((MB, R, D), BF16),
            pltpu.VMEM((MB, C, D), BF16),
            pltpu.VMEM((MB, C, D), BF16),
            pltpu.VMEM((MB, R, D), BF16),
            pltpu.VMEM((MB, R, D), BF16),
            pltpu.VMEM((MB, NX, C, D), BF16),
            pltpu.VMEM((MB, NX, C, D), BF16),
            pltpu.VMEM((MB, C, D), BF16),
            pltpu.VMEM((MB, C, D), BF16),
            pltpu.VMEM((MB, 2, C, D), BF16),
            pltpu.VMEM((MB, 2, C, D), BF16),
            pltpu.VMEM((MB, TP, C, 128), BF16),
            pltpu.VMEM((MB, TP, C, 128), BF16),
            pltpu.VMEM((2, MB, NX, C, 128), BF16),
            pltpu.VMEM((2, MB, NX, C, 128), BF16),
            pltpu.VMEM((MB, TP, R, 128), BF16),
            pltpu.VMEM((TP, MB, R, 128), BF16),
            dma((9,)),
            dma((4,)),
            dma((2, TP)),
            dma((2, TP)),
            dma((2, MB, NX)),
            dma((2, MB, NX)),
            dma((2, MB, NX)),
            dma((2, MB, NX)),
            dma((2, MB, 2)),
            dma((2, MB, 2)),
            dma((2, MB, TP)),
            dma((2, MB, TP)),
        ],
        compiler_params=pltpu.CompilerParams(
            collective_id=0, has_side_effects=True, vmem_limit_bytes=56 * 1024 * 1024
        ),
        name="chain",
    )(acts, cot, *weights, *firsts, *seconds)


def mean(own, other):
    return ((own.astype(F32) + other.astype(F32)) * 0.5).astype(BF16)


def mean_down_kernel(part, rest, rest_moved, *moved_and_out):
    *moved, out = moved_and_out
    moved = [way[...].astype(F32) for way in moved]
    out[:RELAYED, :] = ((part[...].astype(F32) + sum(moved)) * 0.5).astype(BF16)
    out[RELAYED:, :] = mean(rest[...], rest_moved[...])


def mean_down(part, rest, rest_moved, *moved):
    vm = pl.BlockSpec(memory_space=pltpu.VMEM)
    rows = part.shape[0] + rest.shape[0]
    return pl.pallas_call(
        mean_down_kernel,
        out_shape=jax.ShapeDtypeStruct((rows, D), BF16),
        in_specs=[vm] * (3 + len(moved)),
        out_specs=vm,
        cost_estimate=pl.CostEstimate(flops=2 * rows * D, bytes_accessed=6 * rows * D, transcendentals=0),
        name="mean_down",
    )(part, rest, rest_moved, *moved)


def gossip(gate, up, rest, part, distance):
    peers = lax.axis_size("rep")
    onward = [(i, (i + distance) % peers) for i in range(peers)]
    back = [(i, (i - 2) % peers) for i in range(peers) if distance == 2 or i % 2]
    if distance > 2:
        moved = [lax.ppermute(part, "rep", onward)]
    else:
        moved = lax.ppermute(part, "rep", back)
        moved = lax.ppermute(moved, "rep", back)
        if distance == 1:
            last = [(i, (i - 3) % peers) for i in range(peers) if i % 2]
            within = [(i, i + 1) for i in range(peers) if i % 2 == 0]
            moved = [lax.ppermute(moved, "rep", last), lax.ppermute(part, "rep", within)]
        else:
            moved = [lax.ppermute(moved, "rep", back)]
    pairs = []
    for own in (gate, rest, up):
        pairs.append((own, lax.ppermute(own, "rep", onward)))
    new_gate, new_up = mean(*pairs[0]), mean(*pairs[2])
    new_down = mean_down(part, *pairs[1], *moved)
    return lax.optimization_barrier((new_gate, new_up, new_down))


def on_device(
    acts, cotangent, w_gate, w_up, w_down, m_gate, m_up, m_down, v_gate, v_up, v_down, steps
):
    def by_units(gate, up, down):
        return gate[0, 0].T, up[0, 0].T, down[0, 0]

    y, dx, gate, up, part, rest = chain(
        acts[0].T,
        cotangent[0].T,
        by_units(w_gate, w_up, w_down),
        by_units(m_gate, m_up, m_down),
        by_units(v_gate, v_up, v_down),
    )
    levels = lax.axis_size("rep").bit_length() - 1
    branches = [functools.partial(gossip, distance=2**level) for level in range(levels)]
    new_gate, new_up, new_down = lax.switch(
        steps[0] % levels, branches, gate, up, rest, part
    )
    return (
        y.astype(BF16).T[None, None],
        dx.astype(BF16).T[None, None],
        new_gate.T[None, None],
        new_up.T[None, None],
        new_down[None, None],
    )


def solution(mesh):
    return jax.shard_map(
        on_device,
        mesh=mesh,
        in_specs=(
            P("rep", None, "tp"),
            P("rep", None, "tp"),
            P("section", "rep", None, "tp"),
            P("section", "rep", None, "tp"),
            P("section", "rep", "tp", None),
            P("section", "rep", None, "tp"),
            P("section", "rep", None, "tp"),
            P("section", "rep", "tp", None),
            P("section", "rep", None, "tp"),
            P("section", "rep", None, "tp"),
            P("section", "rep", "tp", None),
            P("section"),
        ),
        out_specs=(
            P("section", "rep", None, "tp"),
            P("section", "rep", None, "tp"),
            P("section", "rep", None, "tp"),
            P("section", "rep", None, "tp"),
            P("section", "rep", "tp", None),
        ),
        check_vma=False,
    )
```
